32 devices in a mesh: row: 4 (over y, core), col: 8 (over z, x).
Axes of the slice: x: 2, y: 2, z: 4, core: 2. Of those that a mesh axis runs over, the one named last changes fastest.
Arguments:
- source_desc: bfloat16 [8192, 64], P('row', 'col'), may hold values from -9 to 9
- target_desc: bfloat16 [16384, 64], P('col'), may hold values from -9 to 9
- source_mass: bfloat16 [8192], P('row'), may hold values from 0.099609375 to 10
- target_mass: bfloat16 [16384], P('col'), may hold values from 0.099609375 to 10
Outputs:
- cross_source: float32 [8192], P('row')
- cross_target: float32 [16384], P('col')
- self_source: float32 [8192], P('row')
- self_target: float32 [16384], P('col')
The draws below stay inside these ranges and needn't reach their ends.
All inputs are finite; a program needn't handle non-finite values.
Results may differ from the reference program's by a relative error of at most 0.0003.
Values may be sent and summed in bfloat16 or wider, within the bound.
No kernel may reach another device: no remote copies, remote signals or barrier semaphores. Data moves between devices by JAX's collectives and lax.ppermute only.
A program may use at most 64 MiB of HBM per device.

```python
import math
import jax
import jax.numpy as jnp
from jax import lax

C = 64
ITERS = 2
NX = 8192
NY = 16384


def descriptor_values(key, row_count, residue, offset):
    first_key = jax.random.fold_in(key, 0)
    values = jnp.clip(jax.random.normal(first_key, (row_count, C), jnp.float32), -6.0, 6.0) * (2.0 * C) ** (-0.5)
    position = jnp.arange(row_count, dtype=jnp.float32) / row_count
    factor = jnp.exp(position * math.log(3.0))[:, None]
    values = values * factor
    marked = (jnp.arange(row_count) % 64 == residue).astype(jnp.float32)[:, None]
    values = values + marked * offset
    return values.astype(jnp.bfloat16)


def draw_source_desc(key, part):
    return descriptor_values(key, NX, 5, 1.5)


def draw_target_desc(key, part):
    return descriptor_values(jax.random.fold_in(key, 7), NY, 37, -1.5)


def level_of(own_key, shape, cuts, smallest, top_value):
    factor_of, own = 1.0, jax.random.fold_in(own_key, 6)
    for dim, shards_of in cuts:
        draws = jnp.exp(jax.random.uniform(jax.random.fold_in(own, dim), (shards_of,), jnp.float32, smallest / len(cuts), top_value / len(cuts)))
        factor_of = factor_of * jnp.repeat(draws, shape[dim] // shards_of).reshape([-1 if axis == dim else 1 for axis in range(len(shape))])
    return factor_of


def setup_inputs(seed: int = 0) -> dict:
    key_list = jax.random.split(jax.random.key(seed), 5)
    return {
        "source_desc": draw_source_desc(jax.random.fold_in(key_list[4], 71), 0),
        "target_desc": draw_target_desc(jax.random.fold_in(key_list[4], 71), 0),
        "source_mass": jnp.clip(jnp.exp(math.log(10.0) - 4.609084 * jax.random.uniform(key_list[2], (NX,), jnp.float32) ** level_of(key_list[2], (NX,), ((0, 4),), -0.2, 0.2)), 0.099609375, 10.0).astype(jnp.bfloat16),
        "target_mass": jnp.clip(jnp.exp(math.log(10.0) - 4.609084 * jax.random.uniform(key_list[3], (NY,), jnp.float32) ** level_of(key_list[3], (NY,), ((0, 8),), -0.2, 0.2)), 0.099609375, 10.0).astype(jnp.bfloat16),
    }


EPSILON = 0.25
REACH = 1.0
DAMPING = 1.0 / (1.0 + EPSILON / REACH)


def half_norms(points):
    wide = points.astype(jnp.float32)
    return 0.5 * jnp.sum(wide * wide, axis=1)


def tile_stats(left_desc, right_desc, left_norm, right_norm, left_weight, right_weight, want_rows, want_cols):
    count = left_desc.shape[0]
    block = math.gcd(512, count)
    blocks = count // block
    width = left_desc.shape[1]
    right_count = right_desc.shape[0]
    inputs = (left_desc.reshape(blocks, block, width), left_norm.reshape(blocks, block), left_weight.reshape(blocks, block))

    def advance(carry, pieces):
        piece_desc, piece_norm, piece_weight = pieces
        product = lax.dot_general(piece_desc, right_desc, (((1,), (1,)), ((), ())), preferred_element_type=jnp.float32)
        scaled = (piece_norm[:, None] + right_norm[None, :] - product) / EPSILON
        emitted = ()
        if want_rows:
            row_score = right_weight[None, :] - scaled
            row_top = jnp.max(row_score, axis=1)
            row_total = jnp.sum(jnp.exp(row_score - row_top[:, None]), axis=1)
            emitted = (row_top, row_total)
        if want_cols:
            col_top, col_total = carry
            col_score = piece_weight[:, None] - scaled
            fresh_top = jnp.maximum(col_top, jnp.max(col_score, axis=0))
            col_total = col_total * jnp.exp(col_top - fresh_top) + jnp.sum(jnp.exp(col_score - fresh_top[None, :]), axis=0)
            carry = (fresh_top, col_total)
        return carry, emitted

    if want_cols:
        start = (jnp.full((right_count,), -jnp.inf, jnp.float32), jnp.zeros((right_count,), jnp.float32))
    else:
        start = ()
    carry, emitted = lax.scan(advance, start, inputs)
    rows_out = (emitted[0].reshape(count), emitted[1].reshape(count)) if want_rows else None
    cols_out = carry if want_cols else None
    return rows_out, cols_out


def reference(source_desc, target_desc, source_mass, target_mass):
    source_log = jnp.log(source_mass.astype(jnp.float32))
    target_log = jnp.log(target_mass.astype(jnp.float32))
    source_norm = half_norms(source_desc)
    target_norm = half_norms(target_desc)
    cross_source = jnp.zeros(source_log.shape, jnp.float32)
    cross_target = jnp.zeros(target_log.shape, jnp.float32)
    self_source = jnp.zeros(source_log.shape, jnp.float32)
    self_target = jnp.zeros(target_log.shape, jnp.float32)
    for iteration in range(ITERS):
        cross_rows, cross_cols = tile_stats(source_desc, target_desc, source_norm, target_norm, source_log + cross_source / EPSILON, target_log + cross_target / EPSILON, True, True)
        source_rows, unused_a = tile_stats(source_desc, source_desc, source_norm, source_norm, source_log + self_source / EPSILON, source_log + self_source / EPSILON, True, False)
        target_rows, unused_b = tile_stats(target_desc, target_desc, target_norm, target_norm, target_log + self_target / EPSILON, target_log + self_target / EPSILON, True, False)
        fresh_cs = -EPSILON * (cross_rows[0] + jnp.log(cross_rows[1]))
        fresh_ct = -EPSILON * (cross_cols[0] + jnp.log(cross_cols[1]))
        fresh_ss = -EPSILON * (source_rows[0] + jnp.log(source_rows[1]))
        fresh_st = -EPSILON * (target_rows[0] + jnp.log(target_rows[1]))
        cross_source = 0.5 * cross_source + 0.5 * DAMPING * fresh_cs
        cross_target = 0.5 * cross_target + 0.5 * DAMPING * fresh_ct
        self_source = 0.5 * self_source + 0.5 * DAMPING * fresh_ss
        self_target = 0.5 * self_target + 0.5 * DAMPING * fresh_st
    return (cross_source, cross_target, self_source, self_target)
```

```python
import functools
import math

import jax, jax.numpy as jnp
from jax import lax
from jax.experimental import pallas as pl
from jax.experimental.pallas import tpu as pltpu
from jax.sharding import PartitionSpec as P

EPSILON = 0.25
REACH = 1.0
DAMPING = 1.0 / (1.0 + EPSILON / REACH)

LOG2E = math.log2(math.e)
STRIP = 256

def split3(x):
    hi = x.astype(jnp.bfloat16)
    rest = x - hi.astype(jnp.float32)
    mid = rest.astype(jnp.bfloat16)
    lo = (rest - mid.astype(jnp.float32)).astype(jnp.bfloat16)
    return hi, mid, lo

def fill_lanes(rhs, desc_ref, weight):
    wide = desc_ref[...].astype(jnp.float32)
    ch = wide.shape[0]
    bias = weight - 2.0 * jnp.sum(wide * wide, axis=0, keepdims=True)
    hi, mid, lo = split3(bias)
    n = wide.shape[1]
    rhs[0:ch, :] = (4.0 * wide).astype(jnp.bfloat16)
    rhs[ch:3 * ch, :] = jnp.full((2 * ch, n), -2.0, jnp.bfloat16)
    row = lax.broadcasted_iota(jnp.int32, (ch, n), 0)
    hi, mid, lo = (p.astype(jnp.float32) for p in (hi, mid, lo))
    extra = jnp.where(row == 0, hi, jnp.where(row == 1, mid, jnp.where(row == 2, lo, 0.0)))
    rhs[3 * ch:4 * ch, :] = extra.astype(jnp.bfloat16)

def row_operand(points):
    wide = points.astype(jnp.float32)
    square = wide * wide
    high = square.astype(jnp.bfloat16)
    low = (square - high.astype(jnp.float32)).astype(jnp.bfloat16)
    col = lax.broadcasted_iota(jnp.int32, points.shape, 1)
    ones = jnp.where(col < 3, 1.0, 0.0).astype(jnp.bfloat16)
    return jnp.concatenate([points, high, low, ones], axis=1)

def to_rows(vector):
    pieces = [jnp.broadcast_to(vector[:, k:k + 128], (128, 128)).T for k in range(0, vector.shape[1], 128)]
    return jnp.concatenate(pieces, axis=0)

def to_lanes(block):
    return jnp.concatenate([block[k:k + 128, :].T[0:1, :] for k in range(0, block.shape[0], 128)], axis=1)

def rows_sum_lanes(block):
    return jnp.concatenate([jnp.sum(block[k:k + 128, :].T, axis=0, keepdims=True) for k in range(0, block.shape[0], 128)], axis=1)

def fold_rows(x, op):
    parts = [x[k:k + 8, :] for k in range(0, x.shape[0], 8)]
    while len(parts) > 1:
        parts = [op(parts[i], parts[i + 1]) if i + 1 < len(parts) else parts[i] for i in range(0, len(parts), 2)]
    return parts[0]

def fold_lanes(x, op):
    parts = [x[:, k:k + 128] for k in range(0, x.shape[1], 128)]
    return functools.reduce(op, parts)

def cross_kernel(t_ref, w_ref, s_ref, z_ref, row_ref, col_ref, rhs, fbuf, ctop, csum):
    i = pl.program_id(0)
    n = s_ref.shape[1]
    bt = t_ref.shape[0]

    @pl.when(i == 0)
    def _():
        fill_lanes(rhs, s_ref, z_ref[...])
        ctop[...] = jnp.full(ctop.shape, -jnp.inf, jnp.float32)
        csum[...] = jnp.zeros(csum.shape, jnp.float32)

    lhs = row_operand(t_ref[...])
    wrow = to_rows(w_ref[...])
    wide = jnp.concatenate([wrow, wrow], axis=1)
    rmax = None
    for k in range(0, n, STRIP):
        g = jnp.dot(lhs, rhs[:, k:k + STRIP], preferred_element_type=jnp.float32)
        f = (g + wide) * LOG2E
        fbuf[:, k:k + STRIP] = f
        m = fold_lanes(f, jnp.maximum)
        rmax = m if rmax is None else jnp.maximum(rmax, m)
        top = jnp.max(fold_rows(f, jnp.maximum), axis=0, keepdims=True)
        old = ctop[:, k:k + STRIP]
        new = jnp.maximum(old, top)
        csum[:, k:k + STRIP] = csum[:, k:k + STRIP] * jnp.exp2(old - new)
        ctop[:, k:k + STRIP] = new
    r1 = jnp.max(rmax, axis=1, keepdims=True)
    r = jnp.broadcast_to(r1, (bt, 128))
    racc = jnp.zeros((bt, 128), jnp.float32)
    for k in range(0, n, STRIP):
        for h in range(k, k + STRIP, 128):
            f = fbuf[:, h:h + 128]
            racc = racc + jnp.exp2(f - r)
            e2 = jnp.exp2(f - ctop[0:1, h:h + 128])
            csum[:, h:h + 128] = csum[:, h:h + 128] + fold_rows(e2, jnp.add)
    total = jnp.sum(racc, axis=1, keepdims=True)
    row_ref[...] = to_lanes(jnp.broadcast_to(r1 + jnp.log2(total), (bt, 128)))

    @pl.when(i == pl.num_programs(0) - 1)
    def _():
        col_ref[...] = ctop[0:1, :] + jnp.log2(jnp.sum(csum[...], axis=0, keepdims=True))

def cross_tile(t, w, s, z, block=256):
    nt, ch = t.shape
    n = s.shape[1]
    bt = min(block, nt)
    whole = lambda shape: pl.BlockSpec(shape, lambda i: (0,) * len(shape))
    return pl.pallas_call(
        cross_kernel,
        grid=(nt // bt,),
        in_specs=[pl.BlockSpec((bt, ch), lambda i: (i, 0)), pl.BlockSpec((1, bt), lambda i: (0, i)), whole((ch, n)), whole((1, n))],
        out_specs=[pl.BlockSpec((1, bt), lambda i: (0, i)), whole((1, n))],
        out_shape=[jax.ShapeDtypeStruct((1, nt), jnp.float32), jax.ShapeDtypeStruct((1, n), jnp.float32)],
        scratch_shapes=[pltpu.VMEM((4 * ch, n), jnp.bfloat16), pltpu.VMEM((bt, n), jnp.float32), pltpu.VMEM((8, n), jnp.float32), pltpu.VMEM((8, n), jnp.float32)],
        cost_estimate=pl.CostEstimate(flops=2 * nt * n * 4 * ch, bytes_accessed=4 * (nt + n) * ch, transcendentals=2 * nt * n),
        name="cross_tile",
    )(t, w, s, z)

def self_kernel(u_ref, s_ref, z_ref, e_ref, row_ref, rhs):
    i = pl.program_id(0)
    n = s_ref.shape[1]
    bt = u_ref.shape[0]

    @pl.when(i == 0)
    def _():
        fill_lanes(rhs, s_ref, z_ref[...])

    lhs = row_operand(u_ref[...])
    racc = jnp.zeros((bt, 128), jnp.float32)
    for k in range(0, n, STRIP):
        g = jnp.dot(lhs, rhs[:, k:k + STRIP], preferred_element_type=jnp.float32)
        e = jnp.exp(g)
        racc = racc + fold_lanes(e, jnp.add)
        e_ref[:, k:k + STRIP] = e.astype(jnp.bfloat16)
    row_ref[...] = rows_sum_lanes(racc)

def self_tile(u, s, z, block=256):
    nu, ch = u.shape
    n = s.shape[1]
    bt = min(block, nu)
    whole = lambda shape: pl.BlockSpec(shape, lambda i: (0,) * len(shape))
    return pl.pallas_call(
        self_kernel,
        grid=(nu // bt,),
        in_specs=[pl.BlockSpec((bt, ch), lambda i: (i, 0)), whole((ch, n)), whole((1, n))],
        out_specs=[pl.BlockSpec((bt, n), lambda i: (i, 0)), pl.BlockSpec((1, bt), lambda i: (0, i))],
        out_shape=[jax.ShapeDtypeStruct((nu, n), jnp.bfloat16), jax.ShapeDtypeStruct((1, nu), jnp.float32)],
        scratch_shapes=[pltpu.VMEM((4 * ch, n), jnp.bfloat16)],
        cost_estimate=pl.CostEstimate(flops=2 * nu * n * 4 * ch, bytes_accessed=2 * nu * n, transcendentals=nu * n),
        name="self_tile",
    )(u, s, z)

def weigh_kernel(e_ref, w_ref, out_ref, acc):
    i = pl.program_id(0)
    hi, mid, lo = (p.astype(jnp.float32) for p in split3(w_ref[...]))
    row = lax.broadcasted_iota(jnp.int32, (16, hi.shape[1]), 0)
    lhs = jnp.where(row == 0, hi, jnp.where(row == 1, mid, jnp.where(row == 2, lo, 0.0))).astype(jnp.bfloat16)
    part = jnp.dot(lhs, e_ref[...], preferred_element_type=jnp.float32)

    @pl.when(i == 0)
    def _():
        acc[...] = jnp.zeros(acc.shape, jnp.float32)
    acc[...] += part

    @pl.when(i == pl.num_programs(0) - 1)
    def _():
        out_ref[...] = jnp.sum(acc[...], axis=0, keepdims=True)

def weigh_tile(e, w, block=512):
    nu, n = e.shape
    bt = min(block, nu)
    return pl.pallas_call(
        weigh_kernel,
        grid=(nu // bt,),
        in_specs=[pl.BlockSpec((bt, n), lambda i: (i, 0)), pl.BlockSpec((1, bt), lambda i: (0, i))],
        out_specs=pl.BlockSpec((1, n), lambda i: (0, 0)),
        out_shape=jax.ShapeDtypeStruct((1, n), jnp.float32),
        scratch_shapes=[pltpu.VMEM((16, n), jnp.float32)],
        cost_estimate=pl.CostEstimate(flops=2 * nu * n * 16, bytes_accessed=2 * nu * n, transcendentals=0),
        name="weigh_tile",
    )(e, w)


def gather(x, axis):
    count = lax.axis_size(axis)
    return lax.all_to_all(jnp.broadcast_to(x[None], (count,) + x.shape), axis, 0, 0)


def butterfly(value, axis, join):
    count = lax.axis_size(axis)
    step = 1
    while step < count:
        other = lax.ppermute(value, axis, [(i, i ^ step) for i in range(count)])
        value = join(value, other)
        step *= 2
    return value


def join_logs(a, b):
    top = jnp.maximum(a, b)
    return top + jnp.log2(1.0 + jnp.exp2(jnp.minimum(a, b) - top))


def body(source_desc, target_desc, source_mass, target_mass):
    rows = lax.axis_size("row")
    cols = lax.axis_size("col")
    row = lax.axis_index("row")
    col = lax.axis_index("col")
    ns = source_mass.shape[0]
    nt = target_mass.shape[0]
    ps = ns // cols
    pt = nt // rows
    half = DAMPING * EPSILON * 0.5

    def packed(points, mass):
        return jnp.concatenate([points.reshape(-1), mass]).reshape(-1, 128)

    def unpacked(blocks, count):
        flat = blocks.reshape(blocks.shape[0], -1)
        width = flat.shape[1] // count
        points = flat[:, : count * (width - 1)].reshape(-1, width - 1)
        return points, flat[:, count * (width - 1) :].reshape(-1)

    source_lanes = gather(source_desc.T, "col").reshape(-1, ns)
    target_lanes = target_desc.T
    piece = lax.dynamic_slice_in_dim(target_desc, row * pt, pt, 0)
    piece_mass = lax.dynamic_slice_in_dim(target_mass, row * pt, pt, 0)
    target_set, target_set_mass = unpacked(gather(packed(piece, piece_mass), "col"), pt)
    piece = lax.dynamic_slice_in_dim(source_lanes, col * ps, ps, 1).T
    piece_mass = lax.dynamic_slice_in_dim(source_mass, col * ps, ps, 0)
    source_set, source_set_mass = unpacked(gather(packed(piece, piece_mass), "row"), ps)

    smass = source_mass.astype(jnp.float32)
    tmass = target_mass.astype(jnp.float32)
    slog = jnp.log(smass)
    tlog = jnp.log(tmass)

    def join_parts(a, b, logs):
        return jnp.concatenate([join_logs(a[:logs], b[:logs]), a[logs:] + b[logs:]])

    ct_part, cs_part = cross_tile(target_desc, tlog[None], source_lanes, slog[None])
    ss_plan, ss_part = self_tile(source_set, source_lanes, slog[None])
    st_plan, st_part = self_tile(target_set, target_lanes, tlog[None])
    by_col = butterfly(jnp.concatenate([cs_part[0], st_part[0]]), "col", lambda a, b: join_parts(a, b, ns))
    by_row = butterfly(jnp.concatenate([ct_part[0], ss_part[0]]), "row", lambda a, b: join_parts(a, b, nt))
    cross_source = -half * (by_col[:ns] / LOG2E - slog)
    cross_target = -half * (by_row[:nt] / LOG2E - tlog)
    st_set = -half * jnp.log(by_col[ns:])
    ss_set = -half * jnp.log(by_row[nt:])

    z = slog + cross_source / EPSILON
    w = tlog + cross_target / EPSILON
    ct_part, cs_part = cross_tile(target_desc, w[None], source_lanes, z[None])
    ss_part = weigh_tile(ss_plan, (source_set_mass.astype(jnp.float32) * jnp.exp(ss_set / EPSILON))[None])
    st_part = weigh_tile(st_plan, (target_set_mass.astype(jnp.float32) * jnp.exp(st_set / EPSILON))[None])
    ss_own = lax.dynamic_update_slice(
        jnp.zeros((ns,), jnp.float32), lax.dynamic_slice(ss_set, (row * ps,), (ps,)), (col * ps,)
    )
    st_own = lax.dynamic_update_slice(
        jnp.zeros((nt,), jnp.float32), lax.dynamic_slice(st_set, (col * pt,), (pt,)), (row * pt,)
    )
    by_col = butterfly(jnp.concatenate([cs_part[0], ss_part[0], ss_own]), "col", lambda a, b: join_parts(a, b, ns))
    by_row = butterfly(jnp.concatenate([ct_part[0], st_part[0], st_own]), "row", lambda a, b: join_parts(a, b, nt))
    cross_source = 0.5 * cross_source - half * (by_col[:ns] / LOG2E - z)
    cross_target = 0.5 * cross_target - half * (by_row[:nt] / LOG2E - w)
    self_source = 0.5 * by_col[2 * ns :] - half * jnp.log(by_col[ns : 2 * ns] / smass)
    self_target = 0.5 * by_row[2 * nt :] - half * jnp.log(by_row[nt : 2 * nt] / tmass)
    return (cross_source, cross_target, self_source, self_target)


def solution(mesh):
    return jax.shard_map(
        body,
        mesh=mesh,
        in_specs=(P("row", "col"), P("col", None), P("row"), P("col")),
        out_specs=(P("row"), P("col"), P("row"), P("col")),
        check_vma=False,
    )
```

```python
import functools

import jax, jax.numpy as jnp
from jax import lax
from jax.experimental import pallas as pl
from jax.experimental.pallas import tpu as pltpu
from jax.sharding import PartitionSpec as P


EPSILON = 0.25
REACH = 1.0
DAMPING = 1.0 / (1.0 + EPSILON / REACH)

STRIP = 256
EXTRA = 16


def split3(x):
    hi = x.astype(jnp.bfloat16).astype(jnp.float32)
    rest = x - hi
    mid = rest.astype(jnp.bfloat16).astype(jnp.float32)
    return hi, mid, rest - mid


def operand(desc, weight, scale, own):
    wide = desc.astype(jnp.float32)
    bias = weight - 2.0 * jnp.sum(wide * wide, axis=0, keepdims=True)
    hi, mid, lo = split3(bias)
    row = lax.broadcasted_iota(jnp.int32, (EXTRA, wide.shape[1]), 0) - own
    other = jnp.where((row + own >= 3 - own) & (row + own < 6 - own), 1.0, 0.0)
    extra = jnp.where(row == 0, hi, jnp.where(row == 1, mid, jnp.where(row == 2, lo, other)))
    main = desc if scale == 1.0 else (scale * wide).astype(jnp.bfloat16)
    return jnp.concatenate([main, extra.astype(jnp.bfloat16)], axis=0)


def scores(lhs, rhs):
    return lax.dot_general(lhs, rhs, (((0,), (0,)), ((), ())), preferred_element_type=jnp.float32)


def to_lanes(block):
    tiles = [block[k : k + 128, :].T[0:1, :] for k in range(0, block.shape[0], 128)]
    return jnp.concatenate(tiles, axis=1)


def rows_sum_lanes(block):
    tiles = [
        jnp.sum(block[k : k + 128, :].T, axis=0, keepdims=True)
        for k in range(0, block.shape[0], 128)
    ]
    return jnp.concatenate(tiles, axis=1)


def fold_rows(x, op):
    parts = [x[k : k + 8, :] for k in range(0, x.shape[0], 8)]
    while len(parts) > 1:
        pairs = [op(parts[k], parts[k + 1]) for k in range(0, len(parts) - 1, 2)]
        parts = pairs + parts[len(pairs) * 2 :]
    return parts[0]


def fold_lanes(x, op):
    return functools.reduce(op, [x[:, k : k + 128] for k in range(0, x.shape[1], 128)])


def cross_kernel(t_ref, w_ref, s_ref, z_ref, row_ref, col_ref, rhs, fbuf, ctop, csum):
    i = pl.program_id(0)
    n = s_ref.shape[1]
    bt = t_ref.shape[1]

    @pl.when(i == 0)
    def _():
        rhs[...] = operand(s_ref[...], z_ref[...], 4.0, 0)
        ctop[...] = jnp.full(ctop.shape, -jnp.inf, jnp.float32)
        csum[...] = jnp.zeros(csum.shape, jnp.float32)

    lhs = operand(t_ref[...], w_ref[...], 1.0, 3)
    rmax = None
    for k in range(0, n, STRIP):
        f = scores(lhs, rhs[:, k : k + STRIP])
        fbuf[:, k : k + STRIP] = f
        m = fold_lanes(f, jnp.maximum)
        rmax = m if rmax is None else jnp.maximum(rmax, m)
        top = jnp.max(fold_rows(f, jnp.maximum), axis=0, keepdims=True)
        old = ctop[:, k : k + STRIP]
        new = jnp.maximum(old, top)
        csum[:, k : k + STRIP] = csum[:, k : k + STRIP] * jnp.exp(old - new)
        ctop[:, k : k + STRIP] = new
    r1 = jnp.max(rmax, axis=1, keepdims=True)
    r = jnp.broadcast_to(r1, (bt, 128))
    racc = jnp.zeros((bt, 128), jnp.float32)
    for h in range(0, n, 128):
        f = fbuf[:, h : h + 128]
        racc = racc + jnp.exp(f - r)
        e2 = jnp.exp(f - ctop[0:1, h : h + 128])
        csum[:, h : h + 128] = csum[:, h : h + 128] + fold_rows(e2, jnp.add)
    total = jnp.sum(racc, axis=1, keepdims=True)
    row_ref[...] = to_lanes(jnp.broadcast_to(r1 + jnp.log(total), (bt, 128)))

    @pl.when(i == pl.num_programs(0) - 1)
    def _():
        col_ref[...] = ctop[0:1, :] + jnp.log(jnp.sum(csum[...], axis=0, keepdims=True))


def whole(shape):
    return pl.BlockSpec(shape, lambda *i: (0,) * len(shape))


def cross_tile(t, w, s, z, block=256):
    ch, nt = t.shape
    n = s.shape[1]
    bt = min(block, nt)
    return pl.pallas_call(
        cross_kernel,
        grid=(nt // bt,),
        in_specs=[
            pl.BlockSpec((ch, bt), lambda i: (0, i)),
            pl.BlockSpec((1, bt), lambda i: (0, i)),
            whole((ch, n)),
            whole((1, n)),
        ],
        out_specs=[pl.BlockSpec((1, bt), lambda i: (0, i)), whole((1, n))],
        out_shape=[jax.ShapeDtypeStruct((1, k), jnp.float32) for k in (nt, n)],
        scratch_shapes=[
            pltpu.VMEM((ch + EXTRA, n), jnp.bfloat16),
            pltpu.VMEM((bt, n), jnp.float32),
            pltpu.VMEM((8, n), jnp.float32),
            pltpu.VMEM((8, n), jnp.float32),
        ],
        cost_estimate=pl.CostEstimate(
            flops=8 * nt * n * ch, bytes_accessed=4 * (nt + n) * ch, transcendentals=2 * nt * n
        ),
        name="cross_tile",
    )(t, w, s, z)


def self_kernel(flip, u_ref, s_ref, z_ref, row_ref, rhs):
    ch, n = s_ref.shape
    bt = u_ref.shape[2]

    @pl.when(pl.program_id(0) == 0)
    def _():
        rhs[...] = operand(s_ref[...], z_ref[...], 4.0, 0)

    lhs = operand(u_ref[0, 0:ch, :], jnp.zeros((1, bt), jnp.float32), 1.0, 3)
    racc = jnp.zeros((bt, 128), jnp.float32)
    for k in range(0, n, STRIP):
        racc = racc + fold_lanes(jnp.exp(scores(lhs, rhs[:, k : k + STRIP])), jnp.add)
    row_ref[...] = rows_sum_lanes(racc)


def again_kernel(flip, u_ref, w_ref, s_ref, col_ref, rhs, csum):
    i = pl.program_id(0)
    ch, n = s_ref.shape

    @pl.when(i == 0)
    def _():
        rhs[...] = operand(s_ref[...], jnp.zeros((1, n), jnp.float32), 4.0, 0)
        csum[...] = jnp.zeros(csum.shape, jnp.float32)

    mass = u_ref[0, ch : ch + 1, :].astype(jnp.float32)
    weight = jnp.log(mass) - 0.5 * DAMPING * jnp.log(w_ref[...])
    lhs = operand(u_ref[0, 0:ch, :], weight, 1.0, 3)
    for k in range(0, n, STRIP):
        part = fold_rows(jnp.exp(scores(lhs, rhs[:, k : k + STRIP])), jnp.add)
        csum[:, k : k + STRIP] = csum[:, k : k + STRIP] + part

    @pl.when(i == pl.num_programs(0) - 1)
    def _():
        col_ref[...] = jnp.sum(csum[...], axis=0, keepdims=True)


def self_cost(u, n):
    pairs = u.shape[0] * u.shape[2] * n
    return pl.CostEstimate(flops=4 * pairs * u.shape[1], bytes_accessed=u.size, transcendentals=pairs)


def self_tile(u, s, z, flip):
    blocks, depth, bt = u.shape
    ch, n = s.shape
    return pl.pallas_call(
        self_kernel,
        grid_spec=pltpu.PrefetchScalarGridSpec(
            num_scalar_prefetch=1,
            grid=(blocks,),
            in_specs=[
                pl.BlockSpec((1, depth, bt), lambda i, f: (i ^ f[0], 0, 0)),
                whole((ch, n)),
                whole((1, n)),
            ],
            out_specs=pl.BlockSpec((1, bt), lambda i, f: (0, i)),
            scratch_shapes=[pltpu.VMEM((ch + EXTRA, n), jnp.bfloat16)],
        ),
        out_shape=jax.ShapeDtypeStruct((1, blocks * bt), jnp.float32),
        cost_estimate=self_cost(u, n),
        name="self_tile",
    )(flip, u, s, z)


def again_tile(u, w, s, flip):
    blocks, depth, bt = u.shape
    ch, n = s.shape
    return pl.pallas_call(
        again_kernel,
        grid_spec=pltpu.PrefetchScalarGridSpec(
            num_scalar_prefetch=1,
            grid=(blocks,),
            in_specs=[
                pl.BlockSpec((1, depth, bt), lambda i, f: (i ^ f[0], 0, 0)),
                pl.BlockSpec((1, bt), lambda i, f: (0, i)),
                whole((ch, n)),
            ],
            out_specs=whole((1, n)),
            scratch_shapes=[
                pltpu.VMEM((ch + EXTRA, n), jnp.bfloat16),
                pltpu.VMEM((8, n), jnp.float32),
            ],
        ),
        out_shape=jax.ShapeDtypeStruct((1, n), jnp.float32),
        cost_estimate=self_cost(u, n),
        name="again_tile",
    )(flip, u, w, s)


def gather(x, axis):
    count = lax.axis_size(axis)
    return lax.all_to_all(jnp.broadcast_to(x[None], (count,) + x.shape), axis, 0, 0)


def collect(x, axis):
    count = lax.axis_size(axis)
    return [x] + [
        lax.ppermute(x, axis, [(i, i ^ k) for i in range(count)]) for k in range(1, count)
    ]


def tree(parts, op):
    while len(parts) > 1:
        parts = [op(parts[k], parts[k + 1]) for k in range(0, len(parts), 2)]
    return parts[0]


def log_sum(parts):
    top = tree(parts, jnp.maximum)
    return top + jnp.log(tree([jnp.exp(part - top) for part in parts], jnp.add))


def body(source_desc, target_desc, source_mass, target_mass):
    rows = lax.axis_size("row")
    cols = lax.axis_size("col")
    row = lax.axis_index("row")
    col = lax.axis_index("col")
    ns = source_mass.shape[0]
    nt = target_mass.shape[0]
    ps = ns // cols
    pt = nt // rows
    half = DAMPING * EPSILON * 0.5

    source_mass = source_mass[None]
    target_mass = target_mass[None]
    target_lanes = target_desc.T
    source_lanes = gather(source_desc.T, "col").reshape(-1, ns)
    piece = jnp.concatenate([target_lanes, target_mass], axis=0)
    piece = lax.dynamic_slice_in_dim(piece, row * pt, pt, 1)
    target_set = gather(piece, "col")
    piece = jnp.concatenate([source_lanes, source_mass], axis=0)
    piece = lax.dynamic_slice_in_dim(piece, col * ps, ps, 1)
    source_set = jnp.stack(collect(piece, "row"))
    flip = row.astype(jnp.int32)[None]
    level = jnp.zeros((1,), jnp.int32)

    smass = source_mass.astype(jnp.float32)
    tmass = target_mass.astype(jnp.float32)
    slog = jnp.log(smass)
    tlog = jnp.log(tmass)

    ct, cs = cross_tile(target_lanes, tlog, source_lanes, slog)
    ss = self_tile(source_set, source_lanes, slog, flip)
    st = self_tile(target_set, target_lanes, tlog, level)
    by_row = collect(jnp.concatenate([ct, ss], axis=1), "row")
    ct = log_sum([part[:, :nt] for part in by_row])
    ss = tree([part[:, nt:] for part in by_row], jnp.add)
    by_col = gather(jnp.concatenate([cs, st], axis=1), "col")
    cs = log_sum([part[:, :ns] for part in by_col])
    st = tree([part[:, ns:] for part in by_col], jnp.add)
    cross_source = -half * (cs - slog)
    cross_target = -half * (ct - tlog)
    z = slog + cross_source / EPSILON
    w = tlog + cross_target / EPSILON
    ct, cs = cross_tile(target_lanes, w, source_lanes, z)
    ss_again = again_tile(source_set, ss, source_lanes, flip)
    st_again = again_tile(target_set, st, target_lanes, level)

    ss_mine = -half * jnp.log(lax.dynamic_slice_in_dim(ss, row * ps, ps, 1))
    st_mine = -half * jnp.log(lax.dynamic_slice_in_dim(st, col * pt, pt, 1))
    by_col = gather(jnp.concatenate([cs, ss_again, ss_mine], axis=1), "col")
    by_row = collect(jnp.concatenate([ct, st_again, st_mine], axis=1), "row")
    cs = log_sum([part[:, :ns] for part in by_col])
    ss_again = tree([part[:, ns : 2 * ns] for part in by_col], jnp.add)
    ss = by_col[:, :, 2 * ns :].reshape(1, ns)
    ct = log_sum([part[:, :nt] for part in by_row])
    st_again = tree([part[:, nt : 2 * nt] for part in by_row], jnp.add)
    st = jnp.zeros((1, nt), jnp.float32)
    for k, part in enumerate(by_row):
        st = lax.dynamic_update_slice(st, part[:, 2 * nt :], (0, (row ^ k) * pt))
    cross_source = 0.5 * cross_source - half * (cs - z)
    cross_target = 0.5 * cross_target - half * (ct - w)
    self_source = 0.5 * ss - half * jnp.log(ss_again)
    self_target = 0.5 * st - half * jnp.log(st_again)
    return (cross_source[0], cross_target[0], self_source[0], self_target[0])


def solution(mesh):
    return jax.shard_map(
        body,
        mesh=mesh,
        in_specs=(P("row", "col"), P("col", None), P("row"), P("col")),
        out_specs=(P("row"), P("col"), P("row"), P("col")),
        check_vma=False,
    )
```

```python
import functools
import math

import jax, jax.numpy as jnp
from jax import lax
from jax.experimental import pallas as pl
from jax.experimental.pallas import tpu as pltpu
from jax.sharding import PartitionSpec as P


EPSILON = 0.25
REACH = 1.0
DAMPING = 1.0 / (1.0 + EPSILON / REACH)

STRIP = 256
EXTRA = 16
GROUP = 1024


def split3(x):
    hi = x.astype(jnp.bfloat16).astype(jnp.float32)
    rest = x - hi
    mid = rest.astype(jnp.bfloat16).astype(jnp.float32)
    return hi, mid, rest - mid


def operand(desc, weight, scale, own):
    wide = desc.astype(jnp.float32)
    bias = weight - 2.0 * jnp.sum(wide * wide, axis=0, keepdims=True)
    hi, mid, lo = split3(bias)
    row = lax.broadcasted_iota(jnp.int32, (EXTRA, wide.shape[1]), 0) - own
    other = jnp.where((row + own >= 3 - own) & (row + own < 6 - own), 1.0, 0.0)
    extra = jnp.where(row == 0, hi, jnp.where(row == 1, mid, jnp.where(row == 2, lo, other)))
    main = desc if scale == 1.0 else (scale * wide).astype(jnp.bfloat16)
    return jnp.concatenate([main, extra.astype(jnp.bfloat16)], axis=0)


def scores(lhs, rhs):
    return lax.dot_general(lhs, rhs, (((0,), (0,)), ((), ())), preferred_element_type=jnp.float32)


def to_lanes(block):
    tiles = [block[k : k + 128, :].T[0:1, :] for k in range(0, block.shape[0], 128)]
    return jnp.concatenate(tiles, axis=1)


def rows_sum_lanes(block):
    tiles = [
        jnp.sum(block[k : k + 128, :].T, axis=0, keepdims=True)
        for k in range(0, block.shape[0], 128)
    ]
    return jnp.concatenate(tiles, axis=1)


def fold_rows(x, op):
    parts = [x[k : k + 8, :] for k in range(0, x.shape[0], 8)]
    while len(parts) > 1:
        pairs = [op(parts[k], parts[k + 1]) for k in range(0, len(parts) - 1, 2)]
        parts = pairs + parts[len(pairs) * 2 :]
    return parts[0]


def fold_lanes(x, op):
    return functools.reduce(op, [x[:, k : k + 128] for k in range(0, x.shape[1], 128)])


def whole(shape):
    return pl.BlockSpec(shape, lambda *i: (0,) * len(shape))


def damped(log_mass, log_total):
    return log_mass - 0.5 * DAMPING * (log_total - log_mass)


def tree(parts, op):
    while len(parts) > 1:
        parts = [op(parts[k], parts[k + 1]) for k in range(0, len(parts), 2)]
    return parts[0]


def log_sum(parts):
    top = tree(parts, jnp.maximum)
    return top + jnp.log(tree([jnp.exp(part - top) for part in parts], jnp.add))


def start_cross(s, z, rhs, ctop, csum):
    rhs[...] = operand(s, z, 4.0, 0)
    ctop[...] = jnp.full(ctop.shape, -jnp.inf, jnp.float32)
    csum[...] = jnp.zeros(csum.shape, jnp.float32)


def cross_block(t, w, rhs, fbuf, ctop, csum):
    n = rhs.shape[1]
    bt = t.shape[1]
    lhs = operand(t, w, 1.0, 3)
    rmax = None
    for k in range(0, n, STRIP):
        f = scores(lhs, rhs[:, k : k + STRIP])
        fbuf[:, k : k + STRIP] = f
        m = fold_lanes(f, jnp.maximum)
        rmax = m if rmax is None else jnp.maximum(rmax, m)
        top = jnp.max(fold_rows(f, jnp.maximum), axis=0, keepdims=True)
        old = ctop[:, k : k + STRIP]
        new = jnp.maximum(old, top)
        csum[:, k : k + STRIP] = csum[:, k : k + STRIP] * jnp.exp(old - new)
        ctop[:, k : k + STRIP] = new
    r1 = jnp.max(rmax, axis=1, keepdims=True)
    r = jnp.broadcast_to(r1, (bt, 128))
    racc = jnp.zeros((bt, 128), jnp.float32)
    for h in range(0, n, 128):
        f = fbuf[:, h : h + 128]
        racc = racc + jnp.exp(f - r)
        e2 = jnp.exp(f - ctop[0:1, h : h + 128])
        csum[:, h : h + 128] = csum[:, h : h + 128] + fold_rows(e2, jnp.add)
    total = jnp.sum(racc, axis=1, keepdims=True)
    return to_lanes(jnp.broadcast_to(r1 + jnp.log(total), (bt, 128)))


def col_logs(ctop, csum):
    return ctop[0:1, :] + jnp.log(jnp.sum(csum[...], axis=0, keepdims=True))


def last_step():
    return pl.program_id(0) == pl.num_programs(0) - 1


def cross_kernel(t_ref, w_ref, s_ref, z_ref, row_ref, col_ref, *scratch):
    rhs, _, ctop, csum = scratch

    @pl.when(pl.program_id(0) == 0)
    def _():
        start_cross(s_ref[...], z_ref[...], rhs, ctop, csum)

    row_ref[...] = cross_block(t_ref[...], w_ref[...], *scratch)

    @pl.when(last_step())
    def _():
        col_ref[...] = col_logs(ctop, csum)


def cross_scratch(ch, bt, n):
    return [
        pltpu.VMEM((ch + EXTRA, n), jnp.bfloat16),
        pltpu.VMEM((bt, n), jnp.float32),
        pltpu.VMEM((8, n), jnp.float32),
        pltpu.VMEM((8, n), jnp.float32),
    ]


def cross_cost(nt, n, ch):
    return pl.CostEstimate(
        flops=8 * nt * n * ch, bytes_accessed=4 * (nt + n) * ch, transcendentals=2 * nt * n
    )


def cross_tile(t, w, s, z):
    ch, nt = t.shape
    n = s.shape[1]
    bt = math.gcd(GROUP, nt)
    lanes = pl.BlockSpec((1, bt), lambda i: (0, i))
    return pl.pallas_call(
        cross_kernel,
        grid=(nt // bt,),
        in_specs=[pl.BlockSpec((ch, bt), lambda i: (0, i)), lanes, whole((ch, n)), whole((1, n))],
        out_specs=[lanes, whole((1, n))],
        out_shape=[jax.ShapeDtypeStruct((1, k), jnp.float32) for k in (nt, n)],
        scratch_shapes=cross_scratch(ch, bt, n),
        cost_estimate=cross_cost(nt, n, ch),
        name="cross_tile",
    )(t, w, s, z)


def cross_again_kernel(count, t_ref, tl_ref, s_ref, sl_ref, cols_ref, more_ref, *refs):
    parts = refs[:count]
    row_ref, w_ref, z_ref, col_ref = refs[count : count + 4]
    scratch = refs[count + 4 :]
    rhs, _, ctop, csum = scratch
    n = s_ref.shape[1]

    @pl.when(pl.program_id(0) == 0)
    def _():
        cs = log_sum([cols_ref[k, :, 0:n] for k in range(cols_ref.shape[0])])
        z = damped(sl_ref[...], cs)
        z_ref[...] = z
        start_cross(s_ref[...], z, rhs, ctop, csum)

    w = damped(tl_ref[...], log_sum([part[0] for part in parts]))
    w_ref[...] = w
    row_ref[...] = cross_block(t_ref[...], w, *scratch)

    @pl.when(last_step())
    def _():
        logs = col_logs(ctop, csum)
        for k in range(col_ref.shape[0]):
            col_ref[k, :, 0:n] = logs
            col_ref[k, :, n:] = more_ref[...]


def cross_again(t, tlog, s, slog, by_col, by_row, more):
    ch, nt = t.shape
    n = s.shape[1]
    bt = math.gcd(GROUP, nt)
    lanes = pl.BlockSpec((1, bt), lambda i: (0, i))
    copies = by_col.shape[0]
    shape = (copies, 1, n + more.shape[1])
    return pl.pallas_call(
        functools.partial(cross_again_kernel, len(by_row)),
        grid=(nt // bt,),
        in_specs=[
            pl.BlockSpec((ch, bt), lambda i: (0, i)),
            lanes,
            whole((ch, n)),
            whole((1, n)),
            whole(by_col.shape),
            whole(more.shape),
        ]
        + [pl.BlockSpec((1, 1, bt), lambda i: (0, 0, i))] * len(by_row),
        out_specs=[lanes, lanes, whole((1, n)), whole(shape)],
        out_shape=[jax.ShapeDtypeStruct(k, jnp.float32) for k in ((1, nt), (1, nt), (1, n), shape)],
        scratch_shapes=cross_scratch(ch, bt, n),
        cost_estimate=cross_cost(nt, n, ch),
        name="cross_again",
    )(t, tlog, s, slog, by_col, more, *by_row)


def points(flip, u_ref, ch):
    group = u_ref.shape[0]
    order = [k ^ (flip[0] & (group - 1)) for k in range(group)]
    return [jnp.concatenate([u_ref[k, a:b, :] for k in order], axis=1) for a, b in ((0, ch), (ch, ch + 1))]


def self_kernel(flip, u_ref, s_ref, z_ref, more_ref, out_ref, rhs):
    i = pl.program_id(0)
    ch, n = s_ref.shape
    extra = more_ref.shape[1]

    @pl.when(i == 0)
    def _():
        rhs[...] = operand(s_ref[...], z_ref[...], 4.0, 0)
        for k in range(out_ref.shape[0]):
            out_ref[k, :, 0:extra] = more_ref[...]

    desc, _ = points(flip, u_ref, ch)
    bt = desc.shape[1]
    lhs = operand(desc, jnp.zeros((1, bt), jnp.float32), 1.0, 3)
    racc = jnp.zeros((bt, 128), jnp.float32)
    for k in range(0, n, STRIP):
        racc = racc + fold_lanes(jnp.exp(scores(lhs, rhs[:, k : k + STRIP])), jnp.add)
    sums = rows_sum_lanes(racc)
    start = pl.multiple_of(extra + i * bt, 128)
    for k in range(out_ref.shape[0]):
        out_ref[k, :, pl.ds(start, bt)] = sums


def self_cost(u, n):
    pairs = u.shape[0] * u.shape[2] * n
    return pl.CostEstimate(flops=4 * pairs * u.shape[1], bytes_accessed=u.size, transcendentals=pairs)


def grouped(u):
    blocks, depth, bt = u.shape
    group = math.gcd(blocks, max(1, GROUP // bt))
    return group, pl.BlockSpec((group, depth, bt), lambda i, f: (i ^ (f[0] // group), 0, 0))


def self_tile(u, s, z, flip, more, copies):
    blocks, _, bt = u.shape
    ch, n = s.shape
    group, block = grouped(u)
    shape = (copies, 1, more.shape[1] + blocks * bt)
    return pl.pallas_call(
        self_kernel,
        grid_spec=pltpu.PrefetchScalarGridSpec(
            num_scalar_prefetch=1,
            grid=(blocks // group,),
            in_specs=[block, whole((ch, n)), whole((1, n)), whole(more.shape)],
            out_specs=whole(shape),
            scratch_shapes=[pltpu.VMEM((ch + EXTRA, n), jnp.bfloat16)],
        ),
        out_shape=jax.ShapeDtypeStruct(shape, jnp.float32),
        cost_estimate=self_cost(u, n),
        name="self_tile",
    )(flip, u, s, z, more)


def again_kernel(skip, ahead, flip, u_ref, s_ref, more_ref, *refs):
    parts, (out_ref, rhs, csum, sums) = refs[:-4], refs[-4:]
    i = pl.program_id(0)
    ch, n = s_ref.shape
    extra = more_ref.shape[1] if ahead else 0
    own = out_ref.shape[2] - extra - n

    @pl.when(i == 0)
    def _():
        rhs[...] = operand(s_ref[...], jnp.zeros((1, n), jnp.float32), 4.0, 0)
        csum[...] = jnp.zeros(csum.shape, jnp.float32)
        pieces = [part[k, :, skip:] for part in parts for k in range(part.shape[0])]
        sums[...] = jnp.log(tree(pieces, jnp.add))
        if ahead:
            out_ref[0, :, 0:extra] = more_ref[...]

    desc, mass = points(flip, u_ref, ch)
    bt = desc.shape[1]
    logs = sums[:, pl.ds(pl.multiple_of(i * bt, 128), bt)]
    weight = jnp.log(mass.astype(jnp.float32)) - 0.5 * DAMPING * logs
    lhs = operand(desc, weight, 1.0, 3)
    for k in range(0, n, STRIP):
        part = fold_rows(jnp.exp(scores(lhs, rhs[:, k : k + STRIP])), jnp.add)
        csum[:, k : k + STRIP] = csum[:, k : k + STRIP] + part

    @pl.when(last_step())
    def _():
        out_ref[0, :, extra : extra + n] = jnp.sum(csum[...], axis=0, keepdims=True)
        mine = sums[:, pl.ds(pl.multiple_of(flip[0] * own, 128), own)]
        out_ref[0, :, extra + n :] = (-0.5 * DAMPING * EPSILON) * mine


def again_tile(u, s, flip, parts, skip, own, more=None):
    blocks, _, bt = u.shape
    ch, n = s.shape
    group, block = grouped(u)
    ahead = more is not None
    if not ahead:
        more = jnp.zeros((1, 128), jnp.float32)
    shape = (1, 1, (more.shape[1] if ahead else 0) + n + own)
    return pl.pallas_call(
        functools.partial(again_kernel, skip, ahead),
        grid_spec=pltpu.PrefetchScalarGridSpec(
            num_scalar_prefetch=1,
            grid=(blocks // group,),
            in_specs=[block, whole((ch, n)), whole(more.shape)] + [whole(part.shape) for part in parts],
            out_specs=whole(shape),
            scratch_shapes=[
                pltpu.VMEM((ch + EXTRA, n), jnp.bfloat16),
                pltpu.VMEM((8, n), jnp.float32),
                pltpu.VMEM((1, blocks * bt), jnp.float32),
            ],
        ),
        out_shape=jax.ShapeDtypeStruct(shape, jnp.float32),
        cost_estimate=self_cost(u, n),
        name="again_tile",
    )(flip, u, s, more, *parts)


def collect(x, axis):
    count = lax.axis_size(axis)
    return [x] + [
        lax.ppermute(x, axis, [(i, i ^ k) for i in range(count)]) for k in range(1, count)
    ]


def near(x, axis):
    count = lax.axis_size(axis)
    return jnp.stack([x, lax.ppermute(x, axis, [(i, i ^ 1) for i in range(count)])])


def far(pair, axis):
    count = lax.axis_size(axis)
    parts = [
        lax.ppermute(pair, axis, [(i, i ^ k) for i in range(count)]) for k in range(2, count, 2)
    ]
    return jnp.concatenate([pair] + parts, axis=0)


def swap(x, axis):
    return lax.all_to_all(x, axis, 0, 0)


def body(source_desc, target_desc, source_mass, target_mass):
    rows = lax.axis_size("row")
    cols = lax.axis_size("col")
    row = lax.axis_index("row")
    col = lax.axis_index("col")
    ns = source_mass.shape[0]
    nt = target_mass.shape[0]
    ps = ns // cols
    pt = nt // rows
    half = DAMPING * EPSILON * 0.5

    source_mass = source_mass[None]
    target_mass = target_mass[None]
    target_lanes = target_desc.T
    blocks = target_lanes.reshape(cols, -1, nt)
    target_swapped = jnp.concatenate(
        [lax.dynamic_index_in_dim(blocks, col ^ k, 0, False) for k in range(cols)], axis=0
    )
    piece = jnp.concatenate([target_lanes, target_mass], axis=0)
    piece = lax.dynamic_slice_in_dim(piece, row * pt, pt, 1)
    pair = near(source_desc.T, "col")
    target_pair = near(piece, "col")
    source_lanes = far(pair, "col").reshape(-1, ns)
    target_set = far(target_pair, "col")
    piece = jnp.concatenate([source_lanes, source_mass], axis=0)
    piece = lax.dynamic_slice_in_dim(piece, col * ps, ps, 1)
    source_set = jnp.stack(collect(piece, "row"))
    flip = row.astype(jnp.int32)[None]
    turn = col.astype(jnp.int32)[None]

    smass = source_mass.astype(jnp.float32)
    tmass = target_mass.astype(jnp.float32)
    slog = jnp.log(smass)
    tlog = jnp.log(tmass)

    ct, cs = cross_tile(target_swapped, tlog, source_lanes, slog)
    sums = self_tile(source_set, source_lanes, slog, flip, ct, 1)
    by_row = collect(sums, "row")
    sums = self_tile(target_set, target_lanes, tlog, turn, cs, cols)
    by_col = swap(sums, "col")
    more = again_tile(source_set, source_lanes, flip, by_row, nt, ps)
    ct, w, z, sums = cross_again(target_swapped, tlog, source_lanes, slog, by_col, by_row, more[0])
    last_col = swap(sums, "col")
    sums = again_tile(target_set, target_lanes, turn, [by_col], ns, pt, ct)
    last_row = [part[0] for part in collect(sums, "row")]

    cs = log_sum([part[:, :ns] for part in last_col])
    ss_again = tree([part[:, ns : 2 * ns] for part in last_col], jnp.add)
    ss = last_col[:, :, 2 * ns :].reshape(1, ns)
    ct = log_sum([part[:, :nt] for part in last_row])
    st_again = tree([part[:, nt : 2 * nt] for part in last_row], jnp.add)
    st = jnp.zeros((1, nt), jnp.float32)
    for k, part in enumerate(last_row):
        st = lax.dynamic_update_slice(st, part[:, 2 * nt :], (0, (row ^ k) * pt))
    cross_source = 0.5 * EPSILON * (z - slog) - half * (cs - z)
    cross_target = 0.5 * EPSILON * (w - tlog) - half * (ct - w)
    self_source = 0.5 * ss - half * jnp.log(ss_again)
    self_target = 0.5 * st - half * jnp.log(st_again)
    return (cross_source[0], cross_target[0], self_source[0], self_target[0])


def solution(mesh):
    return jax.shard_map(
        body,
        mesh=mesh,
        in_specs=(P("row", "col"), P("col", None), P("row"), P("col")),
        out_specs=(P("row"), P("col"), P("row"), P("col")),
        check_vma=False,
    )
```

```python
import functools
import math

import jax, jax.numpy as jnp
from jax import lax
from jax.experimental import pallas as pl
from jax.experimental.pallas import tpu as pltpu
from jax.sharding import PartitionSpec as P


EPSILON = 0.25
REACH = 1.0
DAMPING = 1.0 / (1.0 + EPSILON / REACH)

STRIP = 256
EXTRA = 16
GROUP = 1024
LIMIT = 16 * 2**20


def split3(x):
    hi = x.astype(jnp.bfloat16).astype(jnp.float32)
    rest = x - hi
    mid = rest.astype(jnp.bfloat16).astype(jnp.float32)
    return hi, mid, rest - mid


def operand(desc, weight, scale, own):
    wide = desc.astype(jnp.float32)
    desc = desc.astype(jnp.bfloat16)
    bias = weight - 2.0 * jnp.sum(wide * wide, axis=0, keepdims=True)
    hi, mid, lo = split3(bias)
    row = lax.broadcasted_iota(jnp.int32, (EXTRA, wide.shape[1]), 0) - own
    other = jnp.where((row + own >= 3 - own) & (row + own < 6 - own), 1.0, 0.0)
    extra = jnp.where(row == 0, hi, jnp.where(row == 1, mid, jnp.where(row == 2, lo, other)))
    main = desc if scale == 1.0 else (scale * wide).astype(jnp.bfloat16)
    return jnp.concatenate([main, extra.astype(jnp.bfloat16)], axis=0)


def scores(lhs, rhs):
    return lax.dot_general(lhs, rhs, (((0,), (0,)), ((), ())), preferred_element_type=jnp.float32)


def to_lanes(block):
    tiles = [block[k : k + 128, :].T[0:1, :] for k in range(0, block.shape[0], 128)]
    return jnp.concatenate(tiles, axis=1)


def rows_sum_lanes(block):
    tiles = [
        jnp.sum(block[k : k + 128, :].T, axis=0, keepdims=True)
        for k in range(0, block.shape[0], 128)
    ]
    return jnp.concatenate(tiles, axis=1)


def fold_rows(x, op):
    parts = [x[k : k + 8, :] for k in range(0, x.shape[0], 8)]
    while len(parts) > 1:
        pairs = [op(parts[k], parts[k + 1]) for k in range(0, len(parts) - 1, 2)]
        parts = pairs + parts[len(pairs) * 2 :]
    return parts[0]


def fold_lanes(x, op):
    return functools.reduce(op, [x[:, k : k + 128] for k in range(0, x.shape[1], 128)])


def whole(shape):
    return pl.BlockSpec(shape, lambda *i: (0,) * len(shape))


def damped(log_mass, log_total):
    return log_mass - 0.5 * DAMPING * (log_total - log_mass)


def tree(parts, op):
    while len(parts) > 1:
        parts = [op(parts[k], parts[k + 1]) for k in range(0, len(parts), 2)]
    return parts[0]


def log_sum(parts):
    top = tree(parts, jnp.maximum)
    return top + jnp.log(tree([jnp.exp(part - top) for part in parts], jnp.add))


def start_cross(s, z, rhs, ctop, csum):
    rhs[...] = operand(s, z, 4.0, 0)
    ctop[...] = jnp.full(ctop.shape, -jnp.inf, jnp.float32)
    csum[...] = jnp.zeros(csum.shape, jnp.float32)


def cross_block(t, w, rhs, fbuf, ctop, csum):
    n = rhs.shape[1]
    bt = t.shape[1]
    lhs = operand(t, w, 1.0, 3)
    rmax = None
    for k in range(0, n, STRIP):
        f = scores(lhs, rhs[:, k : k + STRIP])
        fbuf[:, k : k + STRIP] = f
        m = fold_lanes(f, jnp.maximum)
        rmax = m if rmax is None else jnp.maximum(rmax, m)
        top = jnp.max(fold_rows(f, jnp.maximum), axis=0, keepdims=True)
        old = ctop[:, k : k + STRIP]
        new = jnp.maximum(old, top)
        csum[:, k : k + STRIP] = csum[:, k : k + STRIP] * jnp.exp(old - new)
        ctop[:, k : k + STRIP] = new
    r1 = jnp.max(rmax, axis=1, keepdims=True)
    r = jnp.broadcast_to(r1, (bt, 128))
    racc = jnp.zeros((bt, 128), jnp.float32)
    for h in range(0, n, 128):
        f = fbuf[:, h : h + 128]
        racc = racc + jnp.exp(f - r)
        e2 = jnp.exp(f - ctop[0:1, h : h + 128])
        csum[:, h : h + 128] = csum[:, h : h + 128] + fold_rows(e2, jnp.add)
    total = jnp.sum(racc, axis=1, keepdims=True)
    return to_lanes(jnp.broadcast_to(r1 + jnp.log(total), (bt, 128)))


def col_logs(ctop, csum):
    return ctop[0:1, :] + jnp.log(jnp.sum(csum[...], axis=0, keepdims=True))


def last_step():
    return pl.program_id(0) == pl.num_programs(0) - 1


def log_of(mass):
    return jnp.log(mass.astype(jnp.float32))


def swapped(turn, t_ref):
    count = t_ref.shape[0]
    return jnp.concatenate([t_ref[k ^ turn[0]].astype(jnp.float32) for k in range(count)], axis=0)


def cross_kernel(turn, t_ref, w_ref, s_ref, z_ref, row_ref, col_ref, *scratch):
    rhs, _, ctop, csum = scratch

    @pl.when(pl.program_id(0) == 0)
    def _():
        start_cross(s_ref[...], log_of(z_ref[...]), rhs, ctop, csum)

    row_ref[...] = cross_block(swapped(turn, t_ref), log_of(w_ref[...]), *scratch)

    @pl.when(last_step())
    def _():
        col_ref[...] = col_logs(ctop, csum)


def cross_scratch(ch, bt, n):
    return [
        pltpu.VMEM((ch + EXTRA, n), jnp.bfloat16),
        pltpu.VMEM((bt, n), jnp.float32),
        pltpu.VMEM((8, n), jnp.float32),
        pltpu.VMEM((8, n), jnp.float32),
    ]


def cross_cost(nt, n, ch):
    return pl.CostEstimate(
        flops=8 * nt * n * ch, bytes_accessed=4 * (nt + n) * ch, transcendentals=2 * nt * n
    )


def cross_tile(turn, t, w, s, z):
    count, ch, nt = t.shape
    ch = ch * count
    n = s.shape[1]
    bt = math.gcd(GROUP, nt)
    lanes = pl.BlockSpec((1, bt), lambda i, f: (0, i))
    return pl.pallas_call(
        cross_kernel,
        grid_spec=pltpu.PrefetchScalarGridSpec(
            num_scalar_prefetch=1,
            grid=(nt // bt,),
            in_specs=[
                pl.BlockSpec((count, ch // count, bt), lambda i, f: (0, 0, i)),
                lanes,
                whole((ch, n)),
                whole((1, n)),
            ],
            out_specs=[lanes, whole((1, n))],
            scratch_shapes=cross_scratch(ch, bt, n),
        ),
        out_shape=[jax.ShapeDtypeStruct((1, k), jnp.float32) for k in (nt, n)],
        cost_estimate=cross_cost(nt, n, ch),
        compiler_params=pltpu.CompilerParams(vmem_limit_bytes=LIMIT),
        name="cross_tile",
    )(turn, t, w, s, z)


def cross_again_kernel(count, width, turn, t_ref, tm_ref, s_ref, sm_ref, more_ref, *refs):
    parts, cols = refs[:count], refs[count : count + width]
    row_ref, w_ref, z_ref, col_ref = refs[count + width : count + width + 4]
    scratch = refs[count + width + 4 :]
    rhs, _, ctop, csum = scratch
    n = s_ref.shape[1]

    @pl.when(pl.program_id(0) == 0)
    def _():
        z = damped(log_of(sm_ref[...]), log_sum([part[:, 0:n] for part in cols]))
        z_ref[...] = z
        start_cross(s_ref[...], z, rhs, ctop, csum)

    w = damped(log_of(tm_ref[...]), log_sum([part[0] for part in parts]))
    w_ref[...] = w
    row_ref[...] = cross_block(swapped(turn, t_ref), w, *scratch)

    @pl.when(last_step())
    def _():
        logs = col_logs(ctop, csum)
        for k in range(col_ref.shape[0]):
            col_ref[k, :, 0:n] = logs
            col_ref[k, :, n:] = more_ref[...]


def cross_again(turn, t, tmass, s, smass, by_col, by_row, more):
    count, ch, nt = t.shape
    ch = ch * count
    n = s.shape[1]
    bt = math.gcd(GROUP, nt)
    lanes = pl.BlockSpec((1, bt), lambda i, f: (0, i))
    shape = (count, 1, n + more.shape[1])
    return pl.pallas_call(
        functools.partial(cross_again_kernel, len(by_row), len(by_col)),
        grid_spec=pltpu.PrefetchScalarGridSpec(
            num_scalar_prefetch=1,
            grid=(nt // bt,),
            in_specs=[
                pl.BlockSpec((count, ch // count, bt), lambda i, f: (0, 0, i)),
                lanes,
                whole((ch, n)),
                whole((1, n)),
                whole(more.shape),
            ]
            + [pl.BlockSpec((1, 1, bt), lambda i, f: (0, 0, i))] * len(by_row)
            + [whole(part.shape) for part in by_col],
            out_specs=[lanes, lanes, whole((1, n)), whole(shape)],
            scratch_shapes=cross_scratch(ch, bt, n),
        ),
        out_shape=[jax.ShapeDtypeStruct(k, jnp.float32) for k in ((1, nt), (1, nt), (1, n), shape)],
        cost_estimate=cross_cost(nt, n, ch),
        compiler_params=pltpu.CompilerParams(vmem_limit_bytes=LIMIT),
        name="cross_again",
    )(turn, t, tmass, s, smass, more, *by_row, *by_col)


def points(flip, u_ref, ch):
    group = u_ref.shape[0]
    order = [k ^ (flip[0] & (group - 1)) for k in range(group)]
    return [jnp.concatenate([u_ref[k, a:b, :] for k in order], axis=1) for a, b in ((0, ch), (ch, ch + 1))]


def self_kernel(flip, u_ref, s_ref, z_ref, more_ref, out_ref, plan_ref, rhs):
    i = pl.program_id(0)
    ch, n = s_ref.shape
    extra = more_ref.shape[1]

    @pl.when(i == 0)
    def _():
        rhs[...] = operand(s_ref[...], log_of(z_ref[...]), 4.0, 0)
        for k in range(out_ref.shape[0]):
            out_ref[k, :, 0:extra] = more_ref[...]

    desc, _ = points(flip, u_ref, ch)
    bt = desc.shape[1]
    lhs = operand(desc, jnp.zeros((1, bt), jnp.float32), 1.0, 3)
    racc = jnp.zeros((bt, 128), jnp.float32)
    here = pl.ds(pl.multiple_of(i * bt, bt), bt)
    for k in range(0, n, STRIP):
        plan = jnp.exp(scores(lhs, rhs[:, k : k + STRIP]))
        racc = racc + fold_lanes(plan, jnp.add)
        plan_ref[here, k : k + STRIP] = plan.astype(jnp.bfloat16)
    sums = rows_sum_lanes(racc)
    start = pl.multiple_of(extra + i * bt, 128)
    for k in range(out_ref.shape[0]):
        out_ref[k, :, pl.ds(start, bt)] = sums


def self_cost(u, n):
    pairs = u.shape[0] * u.shape[2] * n
    return pl.CostEstimate(flops=4 * pairs * u.shape[1], bytes_accessed=u.size, transcendentals=pairs)


def grouped(u):
    blocks, depth, bt = u.shape
    group = math.gcd(blocks, max(1, GROUP // bt))
    return group, pl.BlockSpec((group, depth, bt), lambda i, f: (i ^ (f[0] // group), 0, 0))


def self_tile(u, s, z, flip, more, copies):
    blocks, _, bt = u.shape
    ch, n = s.shape
    group, block = grouped(u)
    shape = (copies, 1, more.shape[1] + blocks * bt)
    return pl.pallas_call(
        self_kernel,
        grid_spec=pltpu.PrefetchScalarGridSpec(
            num_scalar_prefetch=1,
            grid=(blocks // group,),
            in_specs=[block, whole((ch, n)), whole((1, n)), whole(more.shape)],
            out_specs=[whole(shape), pl.BlockSpec(memory_space=pltpu.VMEM)],
            scratch_shapes=[pltpu.VMEM((ch + EXTRA, n), jnp.bfloat16)],
        ),
        out_shape=[
            jax.ShapeDtypeStruct(shape, jnp.float32),
            jax.ShapeDtypeStruct((blocks * bt, n), jnp.bfloat16),
        ],
        compiler_params=pltpu.CompilerParams(vmem_limit_bytes=LIMIT),
        cost_estimate=self_cost(u, n),
        name="self_tile",
    )(flip, u, s, z, more)


def again_kernel(skip, ahead, place, own, flip, u_ref, z_ref, plan_ref, more_ref, *refs):
    parts, out_ref = refs[:-1], refs[-1]
    rows, n = plan_ref.shape
    extra = more_ref.shape[1] if ahead else 0
    sums = jnp.log(tree([part[:, skip:] if len(part.shape) == 2 else part[0, :, skip:] for part in parts], jnp.add))
    if ahead:
        out_ref[0, :, 0:extra] = more_ref[...]
    blocks, depth, _ = u_ref.shape
    masses = [u_ref[k ^ flip[0], depth - 1 : depth, :] for k in range(blocks)]
    mass = jnp.concatenate(masses, axis=1).astype(jnp.float32)
    weight = mass * jnp.exp(-0.5 * DAMPING * sums)
    hi, mid, lo = split3(weight)
    row = lax.broadcasted_iota(jnp.int32, (EXTRA, rows), 0)
    lhs = jnp.where(row == 0, hi, jnp.where(row == 1, mid, jnp.where(row == 2, lo, 0.0)))
    lhs = lhs.astype(jnp.bfloat16)
    for k in range(0, n, 512):
        acc = jnp.dot(lhs, plan_ref[:, k : k + 512], preferred_element_type=jnp.float32)
        total = jnp.sum(acc, axis=0, keepdims=True) / z_ref[:, k : k + 512].astype(jnp.float32)
        out_ref[0, :, extra + k : extra + k + 512] = total
    last = extra + n
    if place:
        out_ref[0, :, last:] = jnp.zeros((1, out_ref.shape[2] - last), jnp.float32)
        last = pl.multiple_of(last + flip[1] * own, 128)
    for k in range(rows // own):

        @pl.when(flip[0] == k)
        def _():
            mine = (-0.5 * DAMPING * EPSILON) * sums[:, k * own : (k + 1) * own]
            out_ref[0, :, pl.ds(last, own)] = mine


def again_tile(u, z, plan, flip, parts, skip, own, more=None, place=False):
    rows, n = plan.shape
    ahead = more is not None
    if not ahead:
        more = jnp.zeros((1, 128), jnp.float32)
    shape = (1, 1, (more.shape[1] if ahead else 0) + n + (n if place else own))
    vmem = pl.BlockSpec(memory_space=pltpu.VMEM)
    return pl.pallas_call(
        functools.partial(again_kernel, skip, ahead, place, own),
        in_specs=[pl.BlockSpec(memory_space=pltpu.SMEM)] + [vmem] * (4 + len(parts)),
        out_specs=vmem,
        out_shape=jax.ShapeDtypeStruct(shape, jnp.float32),
        compiler_params=pltpu.CompilerParams(vmem_limit_bytes=LIMIT),
        cost_estimate=pl.CostEstimate(flops=32 * rows * n, bytes_accessed=2 * rows * n, transcendentals=0),
        name="again_tile",
    )(flip, u, z, plan, more, *parts)


def collect(x, axis, step=1):
    count = lax.axis_size(axis)
    return [x] + [
        lax.ppermute(x, axis, [(i, i ^ k) for i in range(count)]) for k in range(step, count, step)
    ]


def near(x, axis):
    count = lax.axis_size(axis)
    return jnp.stack([x, lax.ppermute(x, axis, [(i, i ^ 1) for i in range(count)])])


def far(pair, axis):
    count = lax.axis_size(axis)
    parts = [
        lax.ppermute(pair, axis, [(i, i ^ k) for i in range(count)]) for k in range(2, count, 2)
    ]
    return jnp.concatenate([pair] + parts, axis=0)


def swap(x, axis):
    return lax.all_to_all(x, axis, 0, 0)


def body(source_desc, target_desc, source_mass, target_mass):
    rows = lax.axis_size("row")
    cols = lax.axis_size("col")
    row = lax.axis_index("row")
    col = lax.axis_index("col")
    ns = source_mass.shape[0]
    nt = target_mass.shape[0]
    ps = ns // cols
    pt = nt // rows
    half = DAMPING * EPSILON * 0.5

    source_mass = source_mass[None]
    target_mass = target_mass[None]
    target_lanes = target_desc.T
    target_blocks = target_lanes.reshape(cols, -1, nt)
    piece = jnp.concatenate([target_lanes, target_mass], axis=0)
    piece = lax.dynamic_slice_in_dim(piece, row * pt, pt, 1)
    pair = near(source_desc.T, "col")
    target_pair = near(piece, "col")
    source_lanes = far(pair, "col").reshape(-1, ns)
    target_set = far(target_pair, "col")
    piece = jnp.concatenate([source_lanes, source_mass], axis=0)
    piece = lax.dynamic_slice_in_dim(piece, col * ps, ps, 1)
    source_set = jnp.stack(collect(piece, "row"))
    flip = row.astype(jnp.int32)[None]
    turn = col.astype(jnp.int32)[None]
    spot = jnp.stack([col, row]).astype(jnp.int32)

    ct, cs = cross_tile(turn, target_blocks, target_mass, source_lanes, source_mass)
    sums, target_plan = self_tile(target_set, target_lanes, target_mass, turn, cs, 1)
    sums = sums[0]
    other = lax.ppermute(sums, "col", [(i, i ^ 1) for i in range(cols)])
    logs = lax.broadcasted_iota(jnp.int32, sums.shape, 1) < ns
    sums = jnp.where(logs, log_sum([sums, other]), sums + other)
    row_sums, source_plan = self_tile(source_set, source_lanes, source_mass, flip, ct, 1)
    by_row = collect(row_sums, "row")
    by_col = collect(sums, "col", 2)
    more = again_tile(source_set, source_mass, source_plan, flip, by_row, nt, ps)
    ct, w, z, sums = cross_again(
        turn, target_blocks, target_mass, source_lanes, source_mass, by_col, by_row, more[0]
    )
    last_col = swap(sums, "col")
    sums = again_tile(
        target_set, target_mass, target_plan, spot, by_col, ns, pt, ct, True
    )
    last_row = [part[0] for part in collect(sums, "row")]

    slog = jnp.log(source_mass.astype(jnp.float32))
    tlog = jnp.log(target_mass.astype(jnp.float32))
    cs = log_sum([part[:, :ns] for part in last_col])
    ss_again = tree([part[:, ns : 2 * ns] for part in last_col], jnp.add)
    ss = last_col[:, :, 2 * ns :].reshape(1, ns)
    cross_source = 0.5 * EPSILON * (z - slog) - half * (cs - z)
    self_source = 0.5 * ss - half * jnp.log(ss_again)
    ct = log_sum([part[:, :nt] for part in last_row])
    st_again = tree([part[:, nt : 2 * nt] for part in last_row], jnp.add)
    st = tree([part[:, 2 * nt :] for part in last_row], jnp.add)
    cross_target = 0.5 * EPSILON * (w - tlog) - half * (ct - w)
    self_target = 0.5 * st - half * jnp.log(st_again)
    return (cross_source[0], cross_target[0], self_source[0], self_target[0])


def solution(mesh):
    return jax.shard_map(
        body,
        mesh=mesh,
        in_specs=(P("row", "col"), P("col", None), P("row"), P("col")),
        out_specs=(P("row"), P("col"), P("row"), P("col")),
        check_vma=False,
    )
```

```python
import functools
import math

import jax, jax.numpy as jnp
from jax import lax
from jax.experimental import pallas as pl
from jax.experimental.pallas import tpu as pltpu
from jax.sharding import PartitionSpec as P


EPSILON = 0.25
REACH = 1.0
DAMPING = 1.0 / (1.0 + EPSILON / REACH)

STRIP = 256
EXTRA = 16
GROUP = 1024
LIMIT = 16 * 2**20


def split3(x):
    hi = x.astype(jnp.bfloat16).astype(jnp.float32)
    rest = x - hi
    mid = rest.astype(jnp.bfloat16).astype(jnp.float32)
    return hi, mid, rest - mid


def operand(desc, weight, scale, own):
    wide = desc.astype(jnp.float32)
    desc = desc.astype(jnp.bfloat16)
    bias = weight - 2.0 * jnp.sum(wide * wide, axis=0, keepdims=True)
    hi, mid, lo = split3(bias)
    row = lax.broadcasted_iota(jnp.int32, (EXTRA, wide.shape[1]), 0) - own
    other = jnp.where((row + own >= 3 - own) & (row + own < 6 - own), 1.0, 0.0)
    extra = jnp.where(row == 0, hi, jnp.where(row == 1, mid, jnp.where(row == 2, lo, other)))
    main = desc if scale == 1.0 else (scale * wide).astype(jnp.bfloat16)
    return jnp.concatenate([main, extra.astype(jnp.bfloat16)], axis=0)


def scores(lhs, rhs):
    return lax.dot_general(lhs, rhs, (((0,), (0,)), ((), ())), preferred_element_type=jnp.float32)


def to_lanes(block):
    tiles = [block[k : k + 128, :].T[0:1, :] for k in range(0, block.shape[0], 128)]
    return jnp.concatenate(tiles, axis=1)


def rows_sum_lanes(block):
    tiles = [
        jnp.sum(block[k : k + 128, :].T, axis=0, keepdims=True)
        for k in range(0, block.shape[0], 128)
    ]
    return jnp.concatenate(tiles, axis=1)


def fold_rows(x, op):
    parts = [x[k : k + 8, :] for k in range(0, x.shape[0], 8)]
    while len(parts) > 1:
        pairs = [op(parts[k], parts[k + 1]) for k in range(0, len(parts) - 1, 2)]
        parts = pairs + parts[len(pairs) * 2 :]
    return parts[0]


def fold_lanes(x, op):
    return functools.reduce(op, [x[:, k : k + 128] for k in range(0, x.shape[1], 128)])


def whole(shape):
    return pl.BlockSpec(shape, lambda *i: (0,) * len(shape))


def damped(log_mass, log_total):
    return log_mass - 0.5 * DAMPING * (log_total - log_mass)


def kept(log_mass, weight):
    return 0.5 * EPSILON * (weight - log_mass + DAMPING * weight)


def tree(parts, op):
    while len(parts) > 1:
        parts = [op(parts[k], parts[k + 1]) for k in range(0, len(parts), 2)]
    return parts[0]


def log_sum(parts):
    top = tree(parts, jnp.maximum)
    return top + jnp.log(tree([jnp.exp(part - top) for part in parts], jnp.add))


def start_cross(s, z, rhs, ctop, csum):
    rhs[...] = operand(s, z, 4.0, 0)
    ctop[...] = jnp.full(ctop.shape, -jnp.inf, jnp.float32)
    csum[...] = jnp.zeros(csum.shape, jnp.float32)


def cross_block(t, w, rhs, fbuf, ctop, csum):
    n = rhs.shape[1]
    bt = t.shape[1]
    lhs = operand(t, w, 1.0, 3)
    rmax = None
    for k in range(0, n, STRIP):
        f = scores(lhs, rhs[:, k : k + STRIP])
        fbuf[:, k : k + STRIP] = f
        m = fold_lanes(f, jnp.maximum)
        rmax = m if rmax is None else jnp.maximum(rmax, m)
        top = jnp.max(fold_rows(f, jnp.maximum), axis=0, keepdims=True)
        old = ctop[:, k : k + STRIP]
        new = jnp.maximum(old, top)
        csum[:, k : k + STRIP] = csum[:, k : k + STRIP] * jnp.exp(old - new)
        ctop[:, k : k + STRIP] = new
    r1 = jnp.max(rmax, axis=1, keepdims=True)
    r = jnp.broadcast_to(r1, (bt, 128))
    racc = jnp.zeros((bt, 128), jnp.float32)
    for h in range(0, n, 128):
        f = fbuf[:, h : h + 128]
        racc = racc + jnp.exp(f - r)
        e2 = jnp.exp(f - ctop[0:1, h : h + 128])
        csum[:, h : h + 128] = csum[:, h : h + 128] + fold_rows(e2, jnp.add)
    total = jnp.sum(racc, axis=1, keepdims=True)
    return to_lanes(jnp.broadcast_to(r1 + jnp.log(total), (bt, 128)))


def col_logs(ctop, csum):
    return ctop[0:1, :] + jnp.log(jnp.sum(csum[...], axis=0, keepdims=True))


def last_step():
    return pl.program_id(0) == pl.num_programs(0) - 1


def log_of(mass):
    return jnp.log(mass.astype(jnp.float32))


def swapped(turn, t_ref):
    count = t_ref.shape[0]
    return jnp.concatenate([t_ref[k ^ turn[0]].astype(jnp.float32) for k in range(count)], axis=0)


def cross_kernel(turn, t_ref, w_ref, s_ref, z_ref, row_ref, col_ref, *scratch):
    rhs, _, ctop, csum = scratch

    @pl.when(pl.program_id(0) == 0)
    def _():
        start_cross(s_ref[...], log_of(z_ref[...]), rhs, ctop, csum)

    row_ref[...] = cross_block(swapped(turn, t_ref), log_of(w_ref[...]), *scratch)

    @pl.when(last_step())
    def _():
        col_ref[...] = col_logs(ctop, csum)


def cross_scratch(ch, bt, n):
    return [
        pltpu.VMEM((ch + EXTRA, n), jnp.bfloat16),
        pltpu.VMEM((bt, n), jnp.float32),
        pltpu.VMEM((8, n), jnp.float32),
        pltpu.VMEM((8, n), jnp.float32),
    ]


def cross_cost(nt, n, ch):
    return pl.CostEstimate(
        flops=8 * nt * n * ch, bytes_accessed=4 * (nt + n) * ch, transcendentals=2 * nt * n
    )


def cross_tile(turn, t, w, s, z):
    count, ch, nt = t.shape
    ch = ch * count
    n = s.shape[1]
    bt = math.gcd(GROUP, nt)
    lanes = pl.BlockSpec((1, bt), lambda i, f: (0, i))
    return pl.pallas_call(
        cross_kernel,
        grid_spec=pltpu.PrefetchScalarGridSpec(
            num_scalar_prefetch=1,
            grid=(nt // bt,),
            in_specs=[
                pl.BlockSpec((count, ch // count, bt), lambda i, f: (0, 0, i)),
                lanes,
                whole((ch, n)),
                whole((1, n)),
            ],
            out_specs=[lanes, whole((1, n))],
            scratch_shapes=cross_scratch(ch, bt, n),
        ),
        out_shape=[jax.ShapeDtypeStruct((1, k), jnp.float32) for k in (nt, n)],
        cost_estimate=cross_cost(nt, n, ch),
        compiler_params=pltpu.CompilerParams(vmem_limit_bytes=LIMIT),
        name="cross_tile",
    )(turn, t, w, s, z)


def cross_again_kernel(count, width, turn, t_ref, tm_ref, s_ref, sm_ref, more_ref, rest_ref, *refs):
    parts, cols = refs[:count], refs[count : count + width]
    row_ref, w_ref, z_ref, col_ref = refs[count + width : count + width + 4]
    scratch = refs[count + width + 4 :]
    rhs, _, ctop, csum = scratch
    n = s_ref.shape[1]

    @pl.when(pl.program_id(0) == 0)
    def _():
        log_mass = log_of(sm_ref[...])
        z = damped(log_mass, log_sum([part[:, 0:n] for part in cols]))
        z_ref[...] = kept(log_mass, z)
        start_cross(s_ref[...], z, rhs, ctop, csum)

    log_mass = log_of(tm_ref[...])
    w = damped(log_mass, log_sum([part[0] for part in parts]))
    w_ref[...] = kept(log_mass, w)
    bt = w.shape[1]
    here = pl.ds(pl.multiple_of(pl.program_id(0) * bt, 128), bt)
    row_ref[0, :, here] = cross_block(swapped(turn, t_ref), w, *scratch)

    @pl.when(last_step())
    def _():
        row_ref[0, :, row_ref.shape[2] - rest_ref.shape[1] :] = rest_ref[...]
        logs = col_logs(ctop, csum)
        for k in range(col_ref.shape[0]):
            col_ref[k, :, 0:n] = logs
            col_ref[k, :, n:] = more_ref[...]


def cross_again(turn, t, tmass, s, smass, by_col, by_row, more, rest):
    count, ch, nt = t.shape
    ch = ch * count
    n = s.shape[1]
    bt = math.gcd(GROUP, nt)
    lanes = pl.BlockSpec((1, bt), lambda i, f: (0, i))
    shape = (count, 1, n + more.shape[1])
    long = (1, 1, nt + rest.shape[1])
    return pl.pallas_call(
        functools.partial(cross_again_kernel, len(by_row), len(by_col)),
        grid_spec=pltpu.PrefetchScalarGridSpec(
            num_scalar_prefetch=1,
            grid=(nt // bt,),
            in_specs=[
                pl.BlockSpec((count, ch // count, bt), lambda i, f: (0, 0, i)),
                lanes,
                whole((ch, n)),
                whole((1, n)),
                whole(more.shape),
                whole(rest.shape),
            ]
            + [pl.BlockSpec((1, 1, bt), lambda i, f: (0, 0, i))] * len(by_row)
            + [whole(part.shape) for part in by_col],
            out_specs=[whole(long), lanes, whole((1, n)), whole(shape)],
            scratch_shapes=cross_scratch(ch, bt, n),
        ),
        out_shape=[jax.ShapeDtypeStruct(k, jnp.float32) for k in (long, (1, nt), (1, n), shape)],
        cost_estimate=cross_cost(nt, n, ch),
        compiler_params=pltpu.CompilerParams(vmem_limit_bytes=LIMIT),
        name="cross_again",
    )(turn, t, tmass, s, smass, more, rest, *by_row, *by_col)


def points(flip, u_ref, ch):
    group = u_ref.shape[0]
    order = [k ^ (flip[0] & (group - 1)) for k in range(group)]
    return [jnp.concatenate([u_ref[k, a:b, :] for k in order], axis=1) for a, b in ((0, ch), (ch, ch + 1))]


def self_kernel(flip, u_ref, s_ref, z_ref, more_ref, out_ref, plan_ref, rhs):
    i = pl.program_id(0)
    ch, n = s_ref.shape
    extra = more_ref.shape[1]

    @pl.when(i == 0)
    def _():
        rhs[...] = operand(s_ref[...], log_of(z_ref[...]), 4.0, 0)
        for k in range(out_ref.shape[0]):
            out_ref[k, :, 0:extra] = more_ref[...]

    desc, _ = points(flip, u_ref, ch)
    bt = desc.shape[1]
    lhs = operand(desc, jnp.zeros((1, bt), jnp.float32), 1.0, 3)
    racc = jnp.zeros((bt, 128), jnp.float32)
    here = pl.ds(pl.multiple_of(i * bt, bt), bt)
    for k in range(0, n, STRIP):
        plan = jnp.exp(scores(lhs, rhs[:, k : k + STRIP]))
        racc = racc + fold_lanes(plan, jnp.add)
        plan_ref[here, k : k + STRIP] = plan.astype(jnp.bfloat16)
    sums = rows_sum_lanes(racc)
    start = pl.multiple_of(extra + i * bt, 128)
    for k in range(out_ref.shape[0]):
        out_ref[k, :, pl.ds(start, bt)] = sums


def self_cost(u, n):
    pairs = u.shape[0] * u.shape[2] * n
    return pl.CostEstimate(flops=4 * pairs * u.shape[1], bytes_accessed=u.size, transcendentals=pairs)


def grouped(u):
    blocks, depth, bt = u.shape
    group = math.gcd(blocks, max(1, GROUP // bt))
    return group, pl.BlockSpec((group, depth, bt), lambda i, f: (i ^ (f[0] // group), 0, 0))


def self_tile(u, s, z, flip, more, copies):
    blocks, _, bt = u.shape
    ch, n = s.shape
    group, block = grouped(u)
    shape = (copies, 1, more.shape[1] + blocks * bt)
    return pl.pallas_call(
        self_kernel,
        grid_spec=pltpu.PrefetchScalarGridSpec(
            num_scalar_prefetch=1,
            grid=(blocks // group,),
            in_specs=[block, whole((ch, n)), whole((1, n)), whole(more.shape)],
            out_specs=[whole(shape), pl.BlockSpec(memory_space=pltpu.VMEM)],
            scratch_shapes=[pltpu.VMEM((ch + EXTRA, n), jnp.bfloat16)],
        ),
        out_shape=[
            jax.ShapeDtypeStruct(shape, jnp.float32),
            jax.ShapeDtypeStruct((blocks * bt, n), jnp.bfloat16),
        ],
        compiler_params=pltpu.CompilerParams(vmem_limit_bytes=LIMIT),
        cost_estimate=self_cost(u, n),
        name="self_tile",
    )(flip, u, s, z, more)


def again_kernel(skip, ahead, place, own, flip, u_ref, z_ref, plan_ref, more_ref, *refs):
    parts, out_ref = refs[:-1], refs[-1]
    rows, n = plan_ref.shape
    extra = more_ref.shape[1] if ahead else 0
    sums = jnp.log(tree([part[:, skip:] if len(part.shape) == 2 else part[0, :, skip:] for part in parts], jnp.add))
    if ahead:
        out_ref[0, :, 0:extra] = more_ref[...]
    blocks, depth, _ = u_ref.shape
    masses = [u_ref[k ^ flip[0], depth - 1 : depth, :] for k in range(blocks)]
    mass = jnp.concatenate(masses, axis=1).astype(jnp.float32)
    weight = mass * jnp.exp(-0.5 * DAMPING * sums)
    hi, mid, lo = split3(weight)
    row = lax.broadcasted_iota(jnp.int32, (EXTRA, rows), 0)
    lhs = jnp.where(row == 0, hi, jnp.where(row == 1, mid, jnp.where(row == 2, lo, 0.0)))
    lhs = lhs.astype(jnp.bfloat16)
    for k in range(0, n, 512):
        acc = jnp.dot(lhs, plan_ref[:, k : k + 512], preferred_element_type=jnp.float32)
        total = jnp.sum(acc, axis=0, keepdims=True) / z_ref[:, k : k + 512].astype(jnp.float32)
        out_ref[0, :, extra + k : extra + k + 512] = total
    last = extra + n
    if place:
        out_ref[0, :, last:] = jnp.zeros((1, out_ref.shape[2] - last), jnp.float32)
        last = pl.multiple_of(last + flip[1] * own, 128)
    for k in range(rows // own):

        @pl.when(flip[0] == k)
        def _():
            mine = (-0.5 * DAMPING * EPSILON) * sums[:, k * own : (k + 1) * own]
            out_ref[0, :, pl.ds(last, own)] = mine


def again_tile(u, z, plan, flip, parts, skip, own, more=None, place=False):
    rows, n = plan.shape
    ahead = more is not None
    if not ahead:
        more = jnp.zeros((1, 128), jnp.float32)
    shape = (1, 1, (more.shape[1] if ahead else 0) + n + (n if place else own))
    vmem = pl.BlockSpec(memory_space=pltpu.VMEM)
    return pl.pallas_call(
        functools.partial(again_kernel, skip, ahead, place, own),
        in_specs=[pl.BlockSpec(memory_space=pltpu.SMEM)] + [vmem] * (4 + len(parts)),
        out_specs=vmem,
        out_shape=jax.ShapeDtypeStruct(shape, jnp.float32),
        compiler_params=pltpu.CompilerParams(vmem_limit_bytes=LIMIT),
        cost_estimate=pl.CostEstimate(flops=32 * rows * n, bytes_accessed=2 * rows * n, transcendentals=0),
        name="again_tile",
    )(flip, u, z, plan, more, *parts)


def collect(x, axis, step=1):
    count = lax.axis_size(axis)
    return [x] + [
        lax.ppermute(x, axis, [(i, i ^ k) for i in range(count)]) for k in range(step, count, step)
    ]


def send(x, axis, step):
    count = lax.axis_size(axis)
    return lax.ppermute(x, axis, [(i, i ^ step) for i in range(count)])


def gather(x, axis):
    count = lax.axis_size(axis)
    pair = jnp.stack([x, send(x, axis, 1)])
    return jnp.concatenate([pair] + [send(pair, axis, k) for k in range(2, count, 2)])


def swap(x, axis):
    return lax.all_to_all(x, axis, 0, 0)


def body(source_desc, target_desc, source_mass, target_mass):
    rows = lax.axis_size("row")
    cols = lax.axis_size("col")
    row = lax.axis_index("row")
    col = lax.axis_index("col")
    ns = source_mass.shape[0]
    nt = target_mass.shape[0]
    ps = ns // cols
    pt = nt // rows
    half = DAMPING * EPSILON * 0.5

    target_lanes = target_desc.T
    target_blocks = target_lanes.reshape(cols, -1, nt)
    source_lanes = gather(source_desc.T, "col").reshape(-1, ns)
    piece = jnp.concatenate([target_lanes, target_mass[None]], axis=0)
    piece = lax.dynamic_slice_in_dim(piece, row * pt, pt, 1)
    target_set = gather(piece, "col")
    source_mass = source_mass[None]
    target_mass = target_mass[None]
    piece = jnp.concatenate([source_lanes, source_mass], axis=0)
    piece = lax.dynamic_slice_in_dim(piece, col * ps, ps, 1)
    source_set = jnp.stack(collect(piece, "row"))
    flip = row.astype(jnp.int32)[None]
    turn = col.astype(jnp.int32)[None]
    spot = jnp.stack([col, row]).astype(jnp.int32)

    ct, cs = cross_tile(turn, target_blocks, target_mass, source_lanes, source_mass)
    sums, target_plan = self_tile(target_set, target_lanes, target_mass, turn, cs, 1)
    sums = sums[0]
    other = lax.ppermute(sums, "col", [(i, i ^ 1) for i in range(cols)])
    logs = lax.broadcasted_iota(jnp.int32, sums.shape, 1) < ns
    sums = jnp.where(logs, log_sum([sums, other]), sums + other)
    row_sums, source_plan = self_tile(source_set, source_lanes, source_mass, flip, ct, 1)
    by_row = collect(row_sums, "row")
    by_col = collect(sums, "col", 2)
    more = again_tile(source_set, source_mass, source_plan, flip, by_row, nt, ps)
    again = again_tile(
        target_set, target_mass, target_plan, spot, by_col, ns, pt, place=True
    )
    row_sums, base_target, base_source, sums = cross_again(
        turn,
        target_blocks,
        target_mass,
        source_lanes,
        source_mass,
        by_col,
        by_row,
        more[0],
        again[0],
    )
    last_col = swap(sums, "col")
    last_row = [part[0] for part in collect(row_sums, "row")]

    cs = log_sum([part[:, :ns] for part in last_col])
    ss_again = tree([part[:, ns : 2 * ns] for part in last_col], jnp.add)
    ss = last_col[:, :, 2 * ns :].reshape(1, ns)
    cross_source = base_source - half * cs
    self_source = 0.5 * ss - half * jnp.log(ss_again)
    ct = log_sum([part[:, :nt] for part in last_row])
    st_again = tree([part[:, nt : 2 * nt] for part in last_row], jnp.add)
    st = tree([part[:, 2 * nt :] for part in last_row], jnp.add)
    cross_target = base_target - half * ct
    self_target = 0.5 * st - half * jnp.log(st_again)
    return (cross_source[0], cross_target[0], self_source[0], self_target[0])


def solution(mesh):
    return jax.shard_map(
        body,
        mesh=mesh,
        in_specs=(P("row", "col"), P("col", None), P("row"), P("col")),
        out_specs=(P("row"), P("col"), P("row"), P("col")),
        check_vma=False,
    )
```

```python
import functools
import math

import jax, jax.numpy as jnp
from jax import lax
from jax.experimental import pallas as pl
from jax.experimental.pallas import tpu as pltpu
from jax.sharding import PartitionSpec as P


EPSILON = 0.25
REACH = 1.0
DAMPING = 1.0 / (1.0 + EPSILON / REACH)

STRIP = 256
EXTRA = 16
GROUP = 1024
LIMIT = 16 * 2**20


def split3(x):
    hi = x.astype(jnp.bfloat16).astype(jnp.float32)
    rest = x - hi
    mid = rest.astype(jnp.bfloat16).astype(jnp.float32)
    return hi, mid, rest - mid


def bias_of(desc, weight):
    wide = desc.astype(jnp.float32)
    return weight - 2.0 * jnp.sum(wide * wide, axis=0, keepdims=True)


def extra_rows(bias, own):
    hi, mid, lo = split3(bias)
    row = lax.broadcasted_iota(jnp.int32, (EXTRA, bias.shape[1]), 0) - own
    other = jnp.where((row + own >= 3 - own) & (row + own < 6 - own), 1.0, 0.0)
    extra = jnp.where(row == 0, hi, jnp.where(row == 1, mid, jnp.where(row == 2, lo, other)))
    return extra.astype(jnp.bfloat16)


def operand(desc, weight, scale, own):
    main = (scale * desc.astype(jnp.float32)).astype(jnp.bfloat16)
    return jnp.concatenate([main, extra_rows(bias_of(desc, weight), own)], axis=0)


def scores(lhs, rhs):
    return lax.dot_general(lhs, rhs, (((0,), (0,)), ((), ())), preferred_element_type=jnp.float32)


def to_lanes(block):
    tiles = [block[k : k + 128, :].T[0:1, :] for k in range(0, block.shape[0], 128)]
    return jnp.concatenate(tiles, axis=1)


def rows_sum_lanes(block):
    tiles = [
        jnp.sum(block[k : k + 128, :].T, axis=0, keepdims=True)
        for k in range(0, block.shape[0], 128)
    ]
    return jnp.concatenate(tiles, axis=1)


def fold_rows(x, op):
    parts = [x[k : k + 8, :] for k in range(0, x.shape[0], 8)]
    while len(parts) > 1:
        pairs = [op(parts[k], parts[k + 1]) for k in range(0, len(parts) - 1, 2)]
        parts = pairs + parts[len(pairs) * 2 :]
    return parts[0]


def fold_lanes(x, op):
    return functools.reduce(op, [x[:, k : k + 128] for k in range(0, x.shape[1], 128)])


def whole(shape):
    return pl.BlockSpec(shape, lambda *i: (0,) * len(shape))


def damped(log_mass, log_total):
    return log_mass - 0.5 * DAMPING * (log_total - log_mass)


def kept(log_mass, weight):
    return 0.5 * EPSILON * (weight - log_mass + DAMPING * weight)


def tree(parts, op):
    while len(parts) > 1:
        parts = [op(parts[k], parts[k + 1]) for k in range(0, len(parts), 2)]
    return parts[0]


def log_sum(parts):
    top = tree(parts, jnp.maximum)
    return top + jnp.log(tree([jnp.exp(part - top) for part in parts], jnp.add))


def start_cross(s, z, rhs, low, bias, fbuf, ctop, csum):
    ch = s.shape[0]
    rhs[...] = operand(s, z, 4.0, 0)
    low[0:ch, :] = rhs[0:ch, :]
    bias[...] = bias_of(s, z)
    ctop[...] = jnp.full(ctop.shape, -jnp.inf, jnp.float32)
    csum[...] = jnp.zeros(csum.shape, jnp.float32)


def cross_block(t, w, rhs, low, bias, fbuf, ctop, csum):
    ch = t.shape[0]
    n = rhs.shape[1]
    bt = t.shape[1]
    lhs = operand(t, w, 1.0, 3)
    rmax = None
    for k in range(0, n, STRIP):
        f = scores(lhs, rhs[:, k : k + STRIP])
        fbuf[:, k : k + STRIP] = f
        m = fold_lanes(f, jnp.maximum)
        rmax = m if rmax is None else jnp.maximum(rmax, m)
        top = jnp.max(fold_rows(f, jnp.maximum), axis=0, keepdims=True)
        old = ctop[:, k : k + STRIP]
        new = jnp.maximum(old, top)
        csum[:, k : k + STRIP] = csum[:, k : k + STRIP] * jnp.exp(old - new)
        ctop[:, k : k + STRIP] = new
        low[ch:, k : k + STRIP] = extra_rows(bias[:, k : k + STRIP] - new[0:1, :], 0)
    r1 = jnp.max(rmax, axis=1, keepdims=True)
    r = jnp.broadcast_to(r1, (bt, 128))
    racc = jnp.zeros((bt, 128), jnp.float32)
    for k in range(0, n, STRIP):
        e2 = jnp.exp(scores(lhs, low[:, k : k + STRIP]))
        csum[:, k : k + STRIP] = csum[:, k : k + STRIP] + fold_rows(e2, jnp.add)
        for h in range(k, k + STRIP, 128):
            racc = racc + jnp.exp(fbuf[:, h : h + 128] - r)
    total = jnp.sum(racc, axis=1, keepdims=True)
    return to_lanes(jnp.broadcast_to(r1 + jnp.log(total), (bt, 128)))


def col_logs(ctop, csum):
    return ctop[0:1, :] + jnp.log(jnp.sum(csum[...], axis=0, keepdims=True))


def last_step():
    return pl.program_id(0) == pl.num_programs(0) - 1


def log_of(mass):
    return jnp.log(mass.astype(jnp.float32))


def swapped(turn, t_ref):
    count = t_ref.shape[0]
    return jnp.concatenate([t_ref[k ^ turn[0]].astype(jnp.float32) for k in range(count)], axis=0)


def cross_kernel(turn, t_ref, w_ref, s_ref, z_ref, row_ref, col_ref, *scratch):
    ctop, csum = scratch[-2:]

    @pl.when(pl.program_id(0) == 0)
    def _():
        start_cross(s_ref[...], log_of(z_ref[...]), *scratch)

    row_ref[...] = cross_block(swapped(turn, t_ref), log_of(w_ref[...]), *scratch)

    @pl.when(last_step())
    def _():
        col_ref[...] = col_logs(ctop, csum)


def cross_scratch(ch, bt, n):
    return [
        pltpu.VMEM((ch + EXTRA, n), jnp.bfloat16),
        pltpu.VMEM((ch + EXTRA, n), jnp.bfloat16),
        pltpu.VMEM((1, n), jnp.float32),
        pltpu.VMEM((bt, n), jnp.float32),
        pltpu.VMEM((8, n), jnp.float32),
        pltpu.VMEM((8, n), jnp.float32),
    ]


def cross_cost(nt, n, ch):
    return pl.CostEstimate(
        flops=8 * nt * n * ch, bytes_accessed=4 * (nt + n) * ch, transcendentals=2 * nt * n
    )


def cross_tile(turn, t, w, s, z):
    count, ch, nt = t.shape
    ch = ch * count
    n = s.shape[1]
    bt = math.gcd(GROUP, nt)
    lanes = pl.BlockSpec((1, bt), lambda i, f: (0, i))
    return pl.pallas_call(
        cross_kernel,
        grid_spec=pltpu.PrefetchScalarGridSpec(
            num_scalar_prefetch=1,
            grid=(nt // bt,),
            in_specs=[
                pl.BlockSpec((count, ch // count, bt), lambda i, f: (0, 0, i)),
                lanes,
                whole((ch, n)),
                whole((1, n)),
            ],
            out_specs=[lanes, whole((1, n))],
            scratch_shapes=cross_scratch(ch, bt, n),
        ),
        out_shape=[jax.ShapeDtypeStruct((1, k), jnp.float32) for k in (nt, n)],
        cost_estimate=cross_cost(nt, n, ch),
        compiler_params=pltpu.CompilerParams(vmem_limit_bytes=LIMIT),
        name="cross_tile",
    )(turn, t, w, s, z)


def cross_again_kernel(count, width, turn, t_ref, tm_ref, s_ref, sm_ref, more_ref, rest_ref, *refs):
    parts, cols = refs[:count], refs[count : count + width]
    row_ref, w_ref, z_ref, col_ref = refs[count + width : count + width + 4]
    scratch = refs[count + width + 4 :]
    ctop, csum = scratch[-2:]
    n = s_ref.shape[1]

    @pl.when(pl.program_id(0) == 0)
    def _():
        log_mass = log_of(sm_ref[...])
        z = damped(log_mass, log_sum([part[:, 0:n] for part in cols]))
        z_ref[...] = kept(log_mass, z)
        start_cross(s_ref[...], z, *scratch)

    log_mass = log_of(tm_ref[...])
    w = damped(log_mass, log_sum([part[0] for part in parts]))
    w_ref[...] = kept(log_mass, w)
    bt = w.shape[1]
    here = pl.ds(pl.multiple_of(pl.program_id(0) * bt, 128), bt)
    row_ref[0, :, here] = cross_block(swapped(turn, t_ref), w, *scratch)

    @pl.when(last_step())
    def _():
        row_ref[0, :, row_ref.shape[2] - rest_ref.shape[1] :] = rest_ref[...]
        logs = col_logs(ctop, csum)
        for k in range(col_ref.shape[0]):
            col_ref[k, :, 0:n] = logs
            col_ref[k, :, n:] = more_ref[...]


def cross_again(turn, t, tmass, s, smass, by_col, by_row, more, rest):
    count, ch, nt = t.shape
    ch = ch * count
    n = s.shape[1]
    bt = math.gcd(GROUP, nt)
    lanes = pl.BlockSpec((1, bt), lambda i, f: (0, i))
    shape = (count, 1, n + more.shape[1])
    long = (1, 1, nt + rest.shape[1])
    return pl.pallas_call(
        functools.partial(cross_again_kernel, len(by_row), len(by_col)),
        grid_spec=pltpu.PrefetchScalarGridSpec(
            num_scalar_prefetch=1,
            grid=(nt // bt,),
            in_specs=[
                pl.BlockSpec((count, ch // count, bt), lambda i, f: (0, 0, i)),
                lanes,
                whole((ch, n)),
                whole((1, n)),
                whole(more.shape),
                whole(rest.shape),
            ]
            + [pl.BlockSpec((1, 1, bt), lambda i, f: (0, 0, i))] * len(by_row)
            + [whole(part.shape) for part in by_col],
            out_specs=[whole(long), lanes, whole((1, n)), whole(shape)],
            scratch_shapes=cross_scratch(ch, bt, n),
        ),
        out_shape=[jax.ShapeDtypeStruct(k, jnp.float32) for k in (long, (1, nt), (1, n), shape)],
        cost_estimate=cross_cost(nt, n, ch),
        compiler_params=pltpu.CompilerParams(vmem_limit_bytes=LIMIT),
        name="cross_again",
    )(turn, t, tmass, s, smass, more, rest, *by_row, *by_col)


def points(flip, u_ref, ch):
    group = u_ref.shape[0]
    order = [k ^ (flip[0] & (group - 1)) for k in range(group)]
    return [jnp.concatenate([u_ref[k, a:b, :] for k in order], axis=1) for a, b in ((0, ch), (ch, ch + 1))]


def self_kernel(flip, u_ref, s_ref, z_ref, more_ref, out_ref, plan_ref, rhs):
    i = pl.program_id(0)
    ch, n = s_ref.shape
    extra = more_ref.shape[1]

    @pl.when(i == 0)
    def _():
        rhs[...] = operand(s_ref[...], log_of(z_ref[...]), 4.0, 0)
        for k in range(out_ref.shape[0]):
            out_ref[k, :, 0:extra] = more_ref[...]

    desc, _ = points(flip, u_ref, ch)
    bt = desc.shape[1]
    lhs = operand(desc, jnp.zeros((1, bt), jnp.float32), 1.0, 3)
    racc = jnp.zeros((bt, 128), jnp.float32)
    here = pl.ds(pl.multiple_of(i * bt, bt), bt)
    for k in range(0, n, STRIP):
        plan = jnp.exp(scores(lhs, rhs[:, k : k + STRIP]))
        racc = racc + fold_lanes(plan, jnp.add)
        plan_ref[here, k : k + STRIP] = plan.astype(jnp.bfloat16)
    sums = rows_sum_lanes(racc)
    start = pl.multiple_of(extra + i * bt, 128)
    for k in range(out_ref.shape[0]):
        out_ref[k, :, pl.ds(start, bt)] = sums


def self_cost(u, n):
    pairs = u.shape[0] * u.shape[2] * n
    return pl.CostEstimate(flops=4 * pairs * u.shape[1], bytes_accessed=u.size, transcendentals=pairs)


def grouped(u):
    blocks, depth, bt = u.shape
    group = math.gcd(blocks, max(1, GROUP // bt))
    return group, pl.BlockSpec((group, depth, bt), lambda i, f: (i ^ (f[0] // group), 0, 0))


def self_tile(u, s, z, flip, more, copies):
    blocks, _, bt = u.shape
    ch, n = s.shape
    group, block = grouped(u)
    shape = (copies, 1, more.shape[1] + blocks * bt)
    return pl.pallas_call(
        self_kernel,
        grid_spec=pltpu.PrefetchScalarGridSpec(
            num_scalar_prefetch=1,
            grid=(blocks // group,),
            in_specs=[block, whole((ch, n)), whole((1, n)), whole(more.shape)],
            out_specs=[whole(shape), pl.BlockSpec(memory_space=pltpu.VMEM)],
            scratch_shapes=[pltpu.VMEM((ch + EXTRA, n), jnp.bfloat16)],
        ),
        out_shape=[
            jax.ShapeDtypeStruct(shape, jnp.float32),
            jax.ShapeDtypeStruct((blocks * bt, n), jnp.bfloat16),
        ],
        compiler_params=pltpu.CompilerParams(vmem_limit_bytes=LIMIT),
        cost_estimate=self_cost(u, n),
        name="self_tile",
    )(flip, u, s, z, more)


def again_kernel(skip, ahead, place, own, flip, u_ref, z_ref, plan_ref, more_ref, *refs):
    parts, out_ref = refs[:-1], refs[-1]
    rows, n = plan_ref.shape
    extra = more_ref.shape[1] if ahead else 0
    sums = jnp.log(tree([part[:, skip:] if len(part.shape) == 2 else part[0, :, skip:] for part in parts], jnp.add))
    if ahead:
        out_ref[0, :, 0:extra] = more_ref[...]
    blocks, depth, _ = u_ref.shape
    masses = [u_ref[k ^ flip[0], depth - 1 : depth, :] for k in range(blocks)]
    mass = jnp.concatenate(masses, axis=1).astype(jnp.float32)
    weight = mass * jnp.exp(-0.5 * DAMPING * sums)
    hi, mid, lo = split3(weight)
    row = lax.broadcasted_iota(jnp.int32, (EXTRA, rows), 0)
    lhs = jnp.where(row == 0, hi, jnp.where(row == 1, mid, jnp.where(row == 2, lo, 0.0)))
    lhs = lhs.astype(jnp.bfloat16)
    for k in range(0, n, 512):
        acc = jnp.dot(lhs, plan_ref[:, k : k + 512], preferred_element_type=jnp.float32)
        total = jnp.sum(acc, axis=0, keepdims=True) / z_ref[:, k : k + 512].astype(jnp.float32)
        out_ref[0, :, extra + k : extra + k + 512] = total
    last = extra + n
    if place:
        out_ref[0, :, last:] = jnp.zeros((1, out_ref.shape[2] - last), jnp.float32)
        last = pl.multiple_of(last + flip[1] * own, 128)
    for k in range(rows // own):

        @pl.when(flip[0] == k)
        def _():
            mine = (-0.5 * DAMPING * EPSILON) * sums[:, k * own : (k + 1) * own]
            out_ref[0, :, pl.ds(last, own)] = mine


def again_tile(u, z, plan, flip, parts, skip, own, more=None, place=False):
    rows, n = plan.shape
    ahead = more is not None
    if not ahead:
        more = jnp.zeros((1, 128), jnp.float32)
    shape = (1, 1, (more.shape[1] if ahead else 0) + n + (n if place else own))
    vmem = pl.BlockSpec(memory_space=pltpu.VMEM)
    return pl.pallas_call(
        functools.partial(again_kernel, skip, ahead, place, own),
        in_specs=[pl.BlockSpec(memory_space=pltpu.SMEM)] + [vmem] * (4 + len(parts)),
        out_specs=vmem,
        out_shape=jax.ShapeDtypeStruct(shape, jnp.float32),
        compiler_params=pltpu.CompilerParams(vmem_limit_bytes=LIMIT),
        cost_estimate=pl.CostEstimate(flops=32 * rows * n, bytes_accessed=2 * rows * n, transcendentals=0),
        name="again_tile",
    )(flip, u, z, plan, more, *parts)


def collect(x, axis, step=1):
    count = lax.axis_size(axis)
    return [x] + [
        lax.ppermute(x, axis, [(i, i ^ k) for i in range(count)]) for k in range(step, count, step)
    ]


def send(x, axis, step):
    count = lax.axis_size(axis)
    return lax.ppermute(x, axis, [(i, i ^ step) for i in range(count)])


def gather(x, axis):
    count = lax.axis_size(axis)
    pair = jnp.stack([x, send(x, axis, 1)])
    return jnp.concatenate([pair] + [send(pair, axis, k) for k in range(2, count, 2)])


def swap(x, axis):
    return lax.all_to_all(x, axis, 0, 0)


def body(source_desc, target_desc, source_mass, target_mass):
    rows = lax.axis_size("row")
    cols = lax.axis_size("col")
    row = lax.axis_index("row")
    col = lax.axis_index("col")
    ns = source_mass.shape[0]
    nt = target_mass.shape[0]
    ps = ns // cols
    pt = nt // rows
    half = DAMPING * EPSILON * 0.5

    target_lanes = target_desc.T
    target_blocks = jnp.where(col < cols, target_lanes.reshape(cols, -1, nt), 0)
    target_blocks = lax.optimization_barrier(target_blocks)
    source_lanes = gather(source_desc.T, "col").reshape(-1, ns)
    piece = jnp.concatenate([target_lanes, target_mass[None]], axis=0)
    piece = lax.dynamic_slice_in_dim(piece, row * pt, pt, 1)
    target_set = gather(piece, "col")
    source_mass = source_mass[None]
    target_mass = target_mass[None]
    piece = jnp.concatenate([source_lanes, source_mass], axis=0)
    piece = lax.dynamic_slice_in_dim(piece, col * ps, ps, 1)
    source_set = jnp.stack(collect(piece, "row"))
    flip = row.astype(jnp.int32)[None]
    turn = col.astype(jnp.int32)[None]
    spot = jnp.stack([col, row]).astype(jnp.int32)

    ct, cs = cross_tile(turn, target_blocks, target_mass, source_lanes, source_mass)
    sums, target_plan = self_tile(
        target_set, target_blocks.reshape(-1, nt), target_mass, turn, cs, 1)
    sums = sums[0]
    other = lax.ppermute(sums, "col", [(i, i ^ 1) for i in range(cols)])
    logs = lax.broadcasted_iota(jnp.int32, sums.shape, 1) < ns
    sums = jnp.where(logs, log_sum([sums, other]), sums + other)
    row_sums, source_plan = self_tile(source_set, source_lanes, source_mass, flip, ct, 1)
    by_row = collect(row_sums, "row")
    by_col = collect(sums, "col", 2)
    more = again_tile(source_set, source_mass, source_plan, flip, by_row, nt, ps)
    again = again_tile(
        target_set, target_mass, target_plan, spot, by_col, ns, pt, place=True
    )
    row_sums, base_target, base_source, sums = cross_again(
        turn,
        target_blocks,
        target_mass,
        source_lanes,
        source_mass,
        by_col,
        by_row,
        more[0],
        again[0],
    )
    last_col = swap(sums, "col")
    last_row = [part[0] for part in collect(row_sums, "row")]

    cs = log_sum([part[:, :ns] for part in last_col])
    ss_again = tree([part[:, ns : 2 * ns] for part in last_col], jnp.add)
    ss = last_col[:, :, 2 * ns :].reshape(1, ns)
    cross_source = base_source - half * cs
    self_source = 0.5 * ss - half * jnp.log(ss_again)
    ct = log_sum([part[:, :nt] for part in last_row])
    st_again = tree([part[:, nt : 2 * nt] for part in last_row], jnp.add)
    st = tree([part[:, 2 * nt :] for part in last_row], jnp.add)
    cross_target = base_target - half * ct
    self_target = 0.5 * st - half * jnp.log(st_again)
    return (cross_source[0], cross_target[0], self_source[0], self_target[0])


def solution(mesh):
    return jax.shard_map(
        body,
        mesh=mesh,
        in_specs=(P("row", "col"), P("col", None), P("row"), P("col")),
        out_specs=(P("row"), P("col"), P("row"), P("col")),
        check_vma=False,
    )
```

```python
import functools
import math

import jax, jax.numpy as jnp
from jax import lax
from jax.experimental import pallas as pl
from jax.experimental.pallas import tpu as pltpu
from jax.sharding import PartitionSpec as P


EPSILON = 0.25
REACH = 1.0
DAMPING = 1.0 / (1.0 + EPSILON / REACH)

STRIP = 256
EXTRA = 16
GROUP = 1024
SUB = 256
SPAN = 2048
LIMIT = 16 * 2**20


def split3(x):
    hi = x.astype(jnp.bfloat16).astype(jnp.float32)
    rest = x - hi
    mid = rest.astype(jnp.bfloat16).astype(jnp.float32)
    return hi, mid, rest - mid


def bias_of(desc, weight):
    wide = desc.astype(jnp.float32)
    return weight - 2.0 * jnp.sum(wide * wide, axis=0, keepdims=True)


def extra_rows(bias, own):
    hi, mid, lo = split3(bias)
    row = lax.broadcasted_iota(jnp.int32, (EXTRA, bias.shape[1]), 0) - own
    other = jnp.where((row + own >= 3 - own) & (row + own < 6 - own), 1.0, 0.0)
    extra = jnp.where(row == 0, hi, jnp.where(row == 1, mid, jnp.where(row == 2, lo, other)))
    return extra.astype(jnp.bfloat16)


def operand(desc, weight, scale, own):
    main = (scale * desc.astype(jnp.float32)).astype(jnp.bfloat16)
    return jnp.concatenate([main, extra_rows(bias_of(desc, weight), own)], axis=0)


def scores(lhs, rhs):
    return lax.dot_general(lhs, rhs, (((0,), (0,)), ((), ())), preferred_element_type=jnp.float32)


def to_lanes(block):
    tiles = [block[k : k + 128, :].T[0:1, :] for k in range(0, block.shape[0], 128)]
    return jnp.concatenate(tiles, axis=1)


def rows_sum_lanes(block):
    tiles = [
        jnp.sum(block[k : k + 128, :].T, axis=0, keepdims=True)
        for k in range(0, block.shape[0], 128)
    ]
    return jnp.concatenate(tiles, axis=1)


def fold_rows(x, op):
    parts = [x[k : k + 8, :] for k in range(0, x.shape[0], 8)]
    while len(parts) > 1:
        pairs = [op(parts[k], parts[k + 1]) for k in range(0, len(parts) - 1, 2)]
        parts = pairs + parts[len(pairs) * 2 :]
    return parts[0]


def fold_lanes(x, op):
    return functools.reduce(op, [x[:, k : k + 128] for k in range(0, x.shape[1], 128)])


def whole(shape):
    return pl.BlockSpec(shape, lambda *i: (0,) * len(shape))


def damped(log_mass, log_total):
    return log_mass - 0.5 * DAMPING * (log_total - log_mass)


def kept(log_mass, weight):
    return 0.5 * EPSILON * (weight - log_mass + DAMPING * weight)


def tree(parts, op):
    while len(parts) > 1:
        parts = [op(parts[k], parts[k + 1]) for k in range(0, len(parts), 2)]
    return parts[0]


def log_sum(parts):
    top = tree(parts, jnp.maximum)
    return top + jnp.log(tree([jnp.exp(part - top) for part in parts], jnp.add))


def start_cross(s, z, rhs, low, bias, fbuf, ctop, csum):
    ch = s.shape[0]
    rhs[...] = operand(s, z, 4.0, 0)
    low[0:ch, :] = rhs[0:ch, :]
    bias[...] = bias_of(s, z)
    ctop[...] = jnp.full(ctop.shape, -jnp.inf, jnp.float32)
    csum[...] = jnp.zeros(csum.shape, jnp.float32)


def cross_block(t, w, rhs, low, bias, fbuf, ctop, csum):
    ch = t.shape[0]
    n = rhs.shape[1]
    bt = fbuf.shape[1]
    count = t.shape[1] // bt
    lhs = [operand(t[:, j : j + bt], w[:, j : j + bt], 1.0, 3) for j in range(0, count * bt, bt)]
    rmax = [None] * count

    def first_pass(j, k):
        f = scores(lhs[j], rhs[:, k : k + STRIP])
        fbuf[j % 2, :, k : k + STRIP] = f
        m = fold_lanes(f, jnp.maximum)
        rmax[j] = m if rmax[j] is None else jnp.maximum(rmax[j], m)
        top = jnp.max(fold_rows(f, jnp.maximum), axis=0, keepdims=True)
        old = ctop[:, k : k + STRIP]
        new = jnp.maximum(old, top)
        csum[:, k : k + STRIP] = csum[:, k : k + STRIP] * jnp.exp(old - new)
        ctop[:, k : k + STRIP] = new
        low[ch:, k : k + STRIP] = extra_rows(bias[:, k : k + STRIP] - new[0:1, :], 0)

    for k in range(0, n, STRIP):
        first_pass(0, k)
    rows = []
    for j in range(count):
        r1 = jnp.max(rmax[j], axis=1, keepdims=True)
        r = jnp.broadcast_to(r1, (bt, 128))
        racc = jnp.zeros((bt, 128), jnp.float32)
        for k in range(0, n, STRIP):
            e2 = jnp.exp(scores(lhs[j], low[:, k : k + STRIP]))
            csum[:, k : k + STRIP] = csum[:, k : k + STRIP] + fold_rows(e2, jnp.add)
            for h in range(k, k + STRIP, 128):
                racc = racc + jnp.exp(fbuf[j % 2, :, h : h + 128] - r)
            if j + 1 < count:
                first_pass(j + 1, k)
        total = jnp.sum(racc, axis=1, keepdims=True)
        rows.append(to_lanes(jnp.broadcast_to(r1 + jnp.log(total), (bt, 128))))
    return jnp.concatenate(rows, axis=1)


def col_logs(ctop, csum):
    return ctop[0:1, :] + jnp.log(jnp.sum(csum[...], axis=0, keepdims=True))


def last_step():
    return pl.program_id(0) == pl.num_programs(0) - 1


def log_of(mass):
    return jnp.log(mass.astype(jnp.float32))


def swapped(turn, t_ref):
    count = t_ref.shape[0]
    return jnp.concatenate([t_ref[k ^ turn[0]].astype(jnp.float32) for k in range(count)], axis=0)


def cross_kernel(turn, t_ref, w_ref, s_ref, z_ref, row_ref, col_ref, *scratch):
    ctop, csum = scratch[-2:]

    @pl.when(pl.program_id(0) == 0)
    def _():
        start_cross(s_ref[...], log_of(z_ref[...]), *scratch)

    row_ref[...] = cross_block(swapped(turn, t_ref), log_of(w_ref[...]), *scratch)

    @pl.when(last_step())
    def _():
        col_ref[...] = col_logs(ctop, csum)


def cross_scratch(ch, bt, n):
    return [
        pltpu.VMEM((ch + EXTRA, n), jnp.bfloat16),
        pltpu.VMEM((ch + EXTRA, n), jnp.bfloat16),
        pltpu.VMEM((1, n), jnp.float32),
        pltpu.VMEM((2, math.gcd(SUB, bt), n), jnp.float32),
        pltpu.VMEM((8, n), jnp.float32),
        pltpu.VMEM((8, n), jnp.float32),
    ]


def cross_cost(nt, n, ch):
    return pl.CostEstimate(
        flops=8 * nt * n * ch, bytes_accessed=4 * (nt + n) * ch, transcendentals=2 * nt * n
    )


def cross_tile(turn, t, w, s, z):
    count, ch, nt = t.shape
    ch = ch * count
    n = s.shape[1]
    bt = math.gcd(SPAN, nt)
    lanes = pl.BlockSpec((1, bt), lambda i, f: (0, i))
    return pl.pallas_call(
        cross_kernel,
        grid_spec=pltpu.PrefetchScalarGridSpec(
            num_scalar_prefetch=1,
            grid=(nt // bt,),
            in_specs=[
                pl.BlockSpec((count, ch // count, bt), lambda i, f: (0, 0, i)),
                lanes,
                whole((ch, n)),
                whole((1, n)),
            ],
            out_specs=[lanes, whole((1, n))],
            scratch_shapes=cross_scratch(ch, bt, n),
        ),
        out_shape=[jax.ShapeDtypeStruct((1, k), jnp.float32) for k in (nt, n)],
        cost_estimate=cross_cost(nt, n, ch),
        compiler_params=pltpu.CompilerParams(vmem_limit_bytes=LIMIT),
        name="cross_tile",
    )(turn, t, w, s, z)


def cross_again_kernel(count, width, turn, t_ref, tm_ref, s_ref, sm_ref, more_ref, rest_ref, *refs):
    parts, cols = refs[:count], refs[count : count + width]
    row_ref, w_ref, z_ref, col_ref = refs[count + width : count + width + 4]
    scratch = refs[count + width + 4 :]
    ctop, csum = scratch[-2:]
    n = s_ref.shape[1]

    @pl.when(pl.program_id(0) == 0)
    def _():
        log_mass = log_of(sm_ref[...])
        z = damped(log_mass, log_sum([part[:, 0:n] for part in cols]))
        z_ref[...] = kept(log_mass, z)
        start_cross(s_ref[...], z, *scratch)

    log_mass = log_of(tm_ref[...])
    w = damped(log_mass, log_sum([part[0] for part in parts]))
    w_ref[...] = kept(log_mass, w)
    bt = w.shape[1]
    here = pl.ds(pl.multiple_of(pl.program_id(0) * bt, 128), bt)
    row_ref[0, :, here] = cross_block(swapped(turn, t_ref), w, *scratch)

    @pl.when(last_step())
    def _():
        row_ref[0, :, row_ref.shape[2] - rest_ref.shape[1] :] = rest_ref[...]
        logs = col_logs(ctop, csum)
        for k in range(col_ref.shape[0]):
            col_ref[k, :, 0:n] = logs
            col_ref[k, :, n:] = more_ref[...]


def cross_again(turn, t, tmass, s, smass, by_col, by_row, more, rest):
    count, ch, nt = t.shape
    ch = ch * count
    n = s.shape[1]
    bt = math.gcd(SPAN, nt)
    lanes = pl.BlockSpec((1, bt), lambda i, f: (0, i))
    shape = (count, 1, n + more.shape[1])
    long = (1, 1, nt + rest.shape[1])
    return pl.pallas_call(
        functools.partial(cross_again_kernel, len(by_row), len(by_col)),
        grid_spec=pltpu.PrefetchScalarGridSpec(
            num_scalar_prefetch=1,
            grid=(nt // bt,),
            in_specs=[
                pl.BlockSpec((count, ch // count, bt), lambda i, f: (0, 0, i)),
                lanes,
                whole((ch, n)),
                whole((1, n)),
                whole(more.shape),
                whole(rest.shape),
            ]
            + [pl.BlockSpec((1, 1, bt), lambda i, f: (0, 0, i))] * len(by_row)
            + [whole(part.shape) for part in by_col],
            out_specs=[whole(long), lanes, whole((1, n)), whole(shape)],
            scratch_shapes=cross_scratch(ch, bt, n),
        ),
        out_shape=[jax.ShapeDtypeStruct(k, jnp.float32) for k in (long, (1, nt), (1, n), shape)],
        cost_estimate=cross_cost(nt, n, ch),
        compiler_params=pltpu.CompilerParams(vmem_limit_bytes=LIMIT),
        name="cross_again",
    )(turn, t, tmass, s, smass, more, rest, *by_row, *by_col)


def points(flip, u_ref, ch):
    group = u_ref.shape[0]
    order = [k ^ (flip[0] & (group - 1)) for k in range(group)]
    return [jnp.concatenate([u_ref[k, a:b, :] for k in order], axis=1) for a, b in ((0, ch), (ch, ch + 1))]


def self_kernel(flip, u_ref, s_ref, z_ref, more_ref, out_ref, plan_ref, rhs):
    i = pl.program_id(0)
    ch, n = s_ref.shape
    extra = more_ref.shape[1]

    @pl.when(i == 0)
    def _():
        rhs[...] = operand(s_ref[...], log_of(z_ref[...]), 4.0, 0)
        for k in range(out_ref.shape[0]):
            out_ref[k, :, 0:extra] = more_ref[...]

    desc, _ = points(flip, u_ref, ch)
    bt = desc.shape[1]
    lhs = operand(desc, jnp.zeros((1, bt), jnp.float32), 1.0, 3)
    racc = jnp.zeros((bt, 128), jnp.float32)
    here = pl.ds(pl.multiple_of(i * bt, bt), bt)
    for k in range(0, n, STRIP):
        plan = jnp.exp(scores(lhs, rhs[:, k : k + STRIP]))
        racc = racc + fold_lanes(plan, jnp.add)
        plan_ref[here, k : k + STRIP] = plan.astype(jnp.bfloat16)
    sums = rows_sum_lanes(racc)
    start = pl.multiple_of(extra + i * bt, 128)
    for k in range(out_ref.shape[0]):
        out_ref[k, :, pl.ds(start, bt)] = sums


def self_cost(u, n):
    pairs = u.shape[0] * u.shape[2] * n
    return pl.CostEstimate(flops=4 * pairs * u.shape[1], bytes_accessed=u.size, transcendentals=pairs)


def grouped(u):
    blocks, depth, bt = u.shape
    group = math.gcd(blocks, max(1, GROUP // bt))
    return group, pl.BlockSpec((group, depth, bt), lambda i, f: (i ^ (f[0] // group), 0, 0))


def self_tile(u, s, z, flip, more, copies):
    blocks, _, bt = u.shape
    ch, n = s.shape
    group, block = grouped(u)
    shape = (copies, 1, more.shape[1] + blocks * bt)
    return pl.pallas_call(
        self_kernel,
        grid_spec=pltpu.PrefetchScalarGridSpec(
            num_scalar_prefetch=1,
            grid=(blocks // group,),
            in_specs=[block, whole((ch, n)), whole((1, n)), whole(more.shape)],
            out_specs=[whole(shape), pl.BlockSpec(memory_space=pltpu.VMEM)],
            scratch_shapes=[pltpu.VMEM((ch + EXTRA, n), jnp.bfloat16)],
        ),
        out_shape=[
            jax.ShapeDtypeStruct(shape, jnp.float32),
            jax.ShapeDtypeStruct((blocks * bt, n), jnp.bfloat16),
        ],
        compiler_params=pltpu.CompilerParams(vmem_limit_bytes=LIMIT),
        cost_estimate=self_cost(u, n),
        name="self_tile",
    )(flip, u, s, z, more)


def again_kernel(skip, ahead, place, own, flip, u_ref, z_ref, plan_ref, more_ref, *refs):
    parts, out_ref = refs[:-1], refs[-1]
    rows, n = plan_ref.shape
    extra = more_ref.shape[1] if ahead else 0
    sums = jnp.log(tree([part[:, skip:] if len(part.shape) == 2 else part[0, :, skip:] for part in parts], jnp.add))
    if ahead:
        out_ref[0, :, 0:extra] = more_ref[...]
    blocks, depth, _ = u_ref.shape
    masses = [u_ref[k ^ flip[0], depth - 1 : depth, :] for k in range(blocks)]
    mass = jnp.concatenate(masses, axis=1).astype(jnp.float32)
    weight = mass * jnp.exp(-0.5 * DAMPING * sums)
    hi, mid, lo = split3(weight)
    row = lax.broadcasted_iota(jnp.int32, (EXTRA, rows), 0)
    lhs = jnp.where(row == 0, hi, jnp.where(row == 1, mid, jnp.where(row == 2, lo, 0.0)))
    lhs = lhs.astype(jnp.bfloat16)
    for k in range(0, n, 512):
        acc = jnp.dot(lhs, plan_ref[:, k : k + 512], preferred_element_type=jnp.float32)
        total = jnp.sum(acc, axis=0, keepdims=True) / z_ref[:, k : k + 512].astype(jnp.float32)
        out_ref[0, :, extra + k : extra + k + 512] = total
    last = extra + n
    if place:
        out_ref[0, :, last:] = jnp.zeros((1, out_ref.shape[2] - last), jnp.float32)
        last = pl.multiple_of(last + flip[1] * own, 128)
    for k in range(rows // own):

        @pl.when(flip[0] == k)
        def _():
            mine = (-0.5 * DAMPING * EPSILON) * sums[:, k * own : (k + 1) * own]
            out_ref[0, :, pl.ds(last, own)] = mine


def again_tile(u, z, plan, flip, parts, skip, own, more=None, place=False):
    rows, n = plan.shape
    ahead = more is not None
    if not ahead:
        more = jnp.zeros((1, 128), jnp.float32)
    shape = (1, 1, (more.shape[1] if ahead else 0) + n + (n if place else own))
    vmem = pl.BlockSpec(memory_space=pltpu.VMEM)
    return pl.pallas_call(
        functools.partial(again_kernel, skip, ahead, place, own),
        in_specs=[pl.BlockSpec(memory_space=pltpu.SMEM)] + [vmem] * (4 + len(parts)),
        out_specs=vmem,
        out_shape=jax.ShapeDtypeStruct(shape, jnp.float32),
        compiler_params=pltpu.CompilerParams(vmem_limit_bytes=LIMIT),
        cost_estimate=pl.CostEstimate(flops=32 * rows * n, bytes_accessed=2 * rows * n, transcendentals=0),
        name="again_tile",
    )(flip, u, z, plan, more, *parts)


def collect(x, axis, step=1):
    count = lax.axis_size(axis)
    return [x] + [
        lax.ppermute(x, axis, [(i, i ^ k) for i in range(count)]) for k in range(step, count, step)
    ]


def send(x, axis, step):
    count = lax.axis_size(axis)
    return lax.ppermute(x, axis, [(i, i ^ step) for i in range(count)])


def gather(x, axis):
    count = lax.axis_size(axis)
    pair = jnp.stack([x, send(x, axis, 1)])
    return jnp.concatenate([pair] + [send(pair, axis, k) for k in range(2, count, 2)])


def swap(x, axis):
    return lax.all_to_all(x, axis, 0, 0)


def body(source_desc, target_desc, source_mass, target_mass):
    rows = lax.axis_size("row")
    cols = lax.axis_size("col")
    row = lax.axis_index("row")
    col = lax.axis_index("col")
    ns = source_mass.shape[0]
    nt = target_mass.shape[0]
    ps = ns // cols
    pt = nt // rows
    half = DAMPING * EPSILON * 0.5

    target_lanes = target_desc.T
    target_blocks = jnp.where(col < cols, target_lanes.reshape(cols, -1, nt), 0)
    target_blocks = lax.optimization_barrier(target_blocks)
    source_lanes = gather(source_desc.T, "col").reshape(-1, ns)
    piece = jnp.concatenate([target_lanes, target_mass[None]], axis=0)
    piece = lax.dynamic_slice_in_dim(piece, row * pt, pt, 1)
    target_set = gather(piece, "col")
    source_mass = source_mass[None]
    target_mass = target_mass[None]
    piece = jnp.concatenate([source_lanes, source_mass], axis=0)
    piece = lax.dynamic_slice_in_dim(piece, col * ps, ps, 1)
    source_set = jnp.stack(collect(piece, "row"))
    flip = row.astype(jnp.int32)[None]
    turn = col.astype(jnp.int32)[None]
    spot = jnp.stack([col, row]).astype(jnp.int32)

    ct, cs = cross_tile(turn, target_blocks, target_mass, source_lanes, source_mass)
    sums, target_plan = self_tile(
        target_set, target_blocks.reshape(-1, nt), target_mass, turn, cs, 1)
    sums = sums[0]
    other = lax.ppermute(sums, "col", [(i, i ^ 1) for i in range(cols)])
    logs = lax.broadcasted_iota(jnp.int32, sums.shape, 1) < ns
    sums = jnp.where(logs, log_sum([sums, other]), sums + other)
    row_sums, source_plan = self_tile(source_set, source_lanes, source_mass, flip, ct, 1)
    by_row = collect(row_sums, "row")
    by_col = collect(sums, "col", 2)
    more = again_tile(source_set, source_mass, source_plan, flip, by_row, nt, ps)
    again = again_tile(
        target_set, target_mass, target_plan, spot, by_col, ns, pt, place=True
    )
    row_sums, base_target, base_source, sums = cross_again(
        turn,
        target_blocks,
        target_mass,
        source_lanes,
        source_mass,
        by_col,
        by_row,
        more[0],
        again[0],
    )
    last_col = swap(sums, "col")
    last_row = [part[0] for part in collect(row_sums, "row")]

    cs = log_sum([part[:, :ns] for part in last_col])
    ss_again = tree([part[:, ns : 2 * ns] for part in last_col], jnp.add)
    ss = last_col[:, :, 2 * ns :].reshape(1, ns)
    cross_source = base_source - half * cs
    self_source = 0.5 * ss - half * jnp.log(ss_again)
    ct = log_sum([part[:, :nt] for part in last_row])
    st_again = tree([part[:, nt : 2 * nt] for part in last_row], jnp.add)
    st = tree([part[:, 2 * nt :] for part in last_row], jnp.add)
    cross_target = base_target - half * ct
    self_target = 0.5 * st - half * jnp.log(st_again)
    return (cross_source[0], cross_target[0], self_source[0], self_target[0])


def solution(mesh):
    return jax.shard_map(
        body,
        mesh=mesh,
        in_specs=(P("row", "col"), P("col", None), P("row"), P("col")),
        out_specs=(P("row"), P("col"), P("row"), P("col")),
        check_vma=False,
    )
```
